32 devices in a mesh: dp: 8 (over y, x, core), mp: 4 (over z).
Axes of the slice: x: 2, y: 2, z: 4, core: 2. Of those that a mesh axis runs over, the one named last changes fastest.
Arguments:
- segment_ids: int32 [2048], replicated, may hold values from 0 to 1, never falling along the last dimension, each value on 1 to 1536 neighbouring positions
- queries: bfloat16 [2048, 4096], P('dp', 'mp'), may hold values from -45 to 45
- keys: bfloat16 [2048, 512], P('dp'), may hold values from -45 to 45
- values: bfloat16 [2048, 512], P('dp'), may hold values from -6 to 6
- out_weight: bfloat16 [4096, 8192], P('mp'), may hold values from -0.125 to 0.125
Outputs:
- attn_out: bfloat16 [2048, 8192], P('dp', 'mp')
The draws below stay inside these ranges and needn't reach their ends.
Inputs may be any that keep to these rules, and one draw needn't show every extreme that they name: `segment_ids`: rollout numbers never fall along the tokens; every rollout has 1 to 1536 tokens and one has exactly 1536.
All inputs are finite; a program needn't handle non-finite values.
Results may differ from the reference program's by a relative error of at most 0.014.
Values may be sent and summed in bfloat16 or wider, within the bound.
A program may use at most 64 MiB of HBM per device.

```python
import math
import jax
import jax.numpy as jnp
import numpy as np
from jax import lax

D = 8192
HD = 128
QHEADS = 32
KVHEADS = 4
GROUP = 8
TOKENS = 2048
ROLLOUTS = 2
MAXLEN = 1536
N_MP = 4


def shared_pair(key):
    base_keys = jnp.clip(jax.random.normal(jax.random.fold_in(key, 11), (TOKENS, KVHEADS * HD), jnp.float32), -6.0, 6.0)
    base_queries = jnp.clip(jax.random.normal(jax.random.fold_in(key, 12), (TOKENS, QHEADS * HD), jnp.float32), -6.0, 6.0)
    keys_out = base_keys
    queries_out = base_queries
    return (queries_out, keys_out)


def draw_queries(key, part):
    return shared_pair(key)[0].astype(jnp.bfloat16)


def draw_keys(key, part):
    return shared_pair(key)[1].astype(jnp.bfloat16)


def spiked(values, key, source, target, parts, factor):
    def block_of(axis_at):
        return (jnp.arange(values.shape[axis_at]) // (values.shape[axis_at] // parts)).reshape((-1,) + (1,) * (values.ndim - 1 - axis_at))

    first = jax.random.permutation(key, parts)[block_of(target)]
    other_side = (block_of(target) + parts // 2) % parts
    return jnp.where((block_of(source) == first) | (block_of(source) == other_side), factor * values, values)


def level_of(rng, shape, cuts, smallest, top_value):
    gain, own = 1.0, jax.random.fold_in(rng, 6)
    for position, shards_of in cuts:
        steps = jnp.exp(jax.random.uniform(jax.random.fold_in(own, position), (shards_of,), jnp.float32, smallest / len(cuts), top_value / len(cuts)))
        gain = gain * jnp.repeat(steps, shape[position] // shards_of).reshape([-1 if axis == position else 1 for axis in range(len(shape))])
    return gain


def profile(amount, total, limit, skew):
    loads = [(1 << 20) // math.isqrt(rank ** skew) + 1 for rank in range(2, amount + 1)]
    surplus, holding = total - limit - (amount - 1), [1] * (amount - 1)
    while surplus > 0:
        movable = [i for i in range(amount - 1) if holding[i] < limit]
        pool, left = sum([loads[i] for i in movable]), surplus
        for i in movable:
            extra = min(limit - holding[i], max(1, left * loads[i] // pool), surplus)
            holding[i] = holding[i] + extra
            surplus = surplus - extra
    return np.array([limit] + holding)


def uneven(key, number_of, total, reach, lean):
    if number_of == 2:
        one = jax.random.randint(key, (), max(1, total - reach), min(reach, total - 1) + 1)
        return jnp.stack([one, total - one])
    sizes = jnp.asarray(profile(number_of, total, reach, lean), jnp.int32)
    couples = (number_of - 1) // 2
    giver, sink = sizes[1:1 + 2 * couples:2], sizes[2:2 + 2 * couples:2]
    slack = jnp.minimum(giver - 1, reach - sink)
    passed = jax.random.randint(jax.random.fold_in(key, 1), (couples,), 0, 1 << 20) % (slack + 1)
    sizes = sizes.at[1:1 + 2 * couples:2].set(giver - passed).at[2:2 + 2 * couples:2].set(sink + passed)
    return sizes[jax.random.permutation(jax.random.fold_in(key, 2), number_of)]


def centred(own_key, dims, width, limit, cuts=(), kind=jnp.bfloat16):
    factor_of = level_of(own_key, dims, cuts, -0.22, 0.18) if cuts else 1.0
    result = jax.random.normal(own_key, dims, jnp.float32) * width * factor_of
    return jnp.minimum(jnp.maximum(result, -limit), limit).astype(kind)


def gaussian_with(own_key, shape, scale, most, cuts, heavy, kind=jnp.bfloat16):
    array = scale * jax.random.normal(own_key, shape, jnp.float32)
    if cuts:
        array = array * level_of(own_key, shape, cuts, -0.22, 0.18)
    return jnp.clip(spiked(array, jax.random.fold_in(own_key, 3), *heavy), -most, most).astype(kind)


def setup_inputs(seed: int = 0) -> dict:
    seeds = jax.random.split(jax.random.key(seed), 6)
    segment_ids = jnp.searchsorted(jnp.cumsum(uneven(seeds[0], ROLLOUTS, TOKENS, MAXLEN, 2)), jnp.arange(TOKENS), side="right").astype(jnp.int32)
    queries = draw_queries(jax.random.fold_in(seeds[5], 71), 0)
    keys = draw_keys(jax.random.fold_in(seeds[5], 71), 0)
    values = centred(seeds[3], (TOKENS, KVHEADS * HD), 1.0, 6.0, ((0, 8),))
    out_weight = gaussian_with(seeds[4], (QHEADS * HD, D), (QHEADS * HD) ** -0.5, 0.125, ((0, 4),), (0, 1, 4, 2.0))
    return dict(segment_ids=segment_ids, queries=queries, keys=keys, values=values, out_weight=out_weight)


def reference(segment_ids, queries, keys, values, out_weight):
    score_scale = 1.0 / math.sqrt(HD)
    block_len = math.gcd(TOKENS, 512)
    block_count = TOKENS // block_len
    positions = jnp.arange(TOKENS, dtype=jnp.int32)
    key_heads = keys.astype(jnp.float32).reshape(TOKENS, KVHEADS, HD).transpose(1, 0, 2)
    value_heads = values.astype(jnp.float32).reshape(TOKENS, KVHEADS, HD).transpose(1, 0, 2)

    def one_block(block_index):
        offset = (block_index * block_len).astype(jnp.int32)
        query_rows = lax.dynamic_slice_in_dim(queries, offset, block_len, 0).astype(jnp.float32)
        query_rows = query_rows.reshape(block_len, KVHEADS, GROUP, HD).transpose(1, 0, 2, 3)
        seg_rows = lax.dynamic_slice_in_dim(segment_ids, offset, block_len, 0)
        pos_rows = offset + jnp.arange(block_len, dtype=jnp.int32)
        allowed = (seg_rows[:, None] == segment_ids[None, :]) & (positions[None, :] <= pos_rows[:, None])

        def one_group(group_args):
            group_queries, group_keys, group_values = group_args
            scores = jnp.einsum('tjd,sd->tjs', group_queries, group_keys) * score_scale
            scores = jnp.where(allowed[:, None, :], scores, -1e+30)
            row_max = lax.optimization_barrier(jnp.max(scores, axis=-1, keepdims=True))
            weights = jnp.where(allowed[:, None, :], jnp.exp(scores - row_max), 0.0)
            denominator = lax.optimization_barrier(jnp.sum(weights, axis=-1, keepdims=True))
            rounded = lax.optimization_barrier(weights.astype(jnp.bfloat16)).astype(jnp.float32)
            mixed = jnp.einsum('tjs,sd->tjd', rounded, group_values) / denominator
            return mixed.astype(jnp.bfloat16)
        return lax.map(one_group, (query_rows, key_heads, value_heads))
    attended = lax.map(one_block, jnp.arange(block_count, dtype=jnp.int32))
    attended = attended.transpose(0, 2, 1, 3, 4).reshape(TOKENS, QHEADS * HD)
    per_device = QHEADS * HD // N_MP
    head_blocks = attended.reshape(TOKENS, N_MP, per_device).transpose(1, 0, 2)
    weight_blocks = out_weight.reshape(N_MP, per_device, D)

    def add_block(carry, block_args):
        block_rows, block_weight = block_args
        partial_value = jnp.dot(block_rows, block_weight, preferred_element_type=jnp.float32)
        rounded = lax.optimization_barrier(partial_value.astype(jnp.bfloat16)).astype(jnp.float32)
        return (carry + rounded, None)
    summed, unused = lax.scan(add_block, jnp.zeros((TOKENS, D), jnp.float32), (head_blocks, weight_blocks))
    return summed.astype(jnp.bfloat16)
```

```python
import functools
import math

import jax
import jax.numpy as jnp
from jax import lax
from jax.experimental import pallas as pl
from jax.experimental.pallas import tpu as pltpu
from jax.sharding import PartitionSpec as P

HD = 128
GROUP = 8
LAG = 2
MESH = pl.DeviceIdType.MESH


def pair_kernel(
    n_dp, n_mp, key_span, piece,
    seg_ref, q_ref, k_hbm, v_hbm, w_hbm, out_ref,
    kv, w, w_end, bias, att, far_out, far_in, end_out, end_in, done,
    load_sems, w_sems, kv_send, kv_recv, pass_send, pass_recv,
    wz_send, wz_recv, wy_send, wy_recv, az_send, az_recv,
    own_send, own_recv, ax_send, ax_recv, rel_send, rel_recv,
    far_send, far_recv, end_send, end_recv, fin_send, fin_recv,
):
    rows = q_ref.shape[0]
    heads = q_ref.shape[1] // HD
    tokens = n_dp * rows
    out_cols = out_ref.shape[1]
    depth, quarter = w.shape[1], w.shape[2]
    chips = n_dp // 2
    r_count = rows // piece
    half_items = 2 * r_count
    w_chunks = 4
    chunk = depth // 2 // w_chunks
    dp, mp = lax.axis_index("dp"), lax.axis_index("mp")
    core, chip = dp % 2, dp // 2
    x, y = chip % 2, chip // 2
    partner = dp + 1 - 2 * core
    x_same, x_other = (y * 2 + 1 - x) * 2 + core, (y * 2 + 1 - x) * 2 + 1 - core
    y_same = ((1 - y) * 2 + x) * 2 + core
    first_row = pl.multiple_of(dp * rows, rows)
    left_half = mp < n_mp // 2
    is_end = (mp == 0) | (mp == n_mp - 1)
    is_mid = jnp.logical_not(is_end)
    end_mp = jnp.where(left_half, 0, n_mp - 1)
    mid_mp = jnp.where(left_half, 1, n_mp - 2)
    far_mp = n_mp - 1 - mp
    slot, slot_partner = x * 2 + core, x * 2 + 1 - core
    slot_x, slot_xo = (1 - x) * 2 + core, (1 - x) * 2 + 1 - core

    def remote(src, dst, send, recv, dp_to=None, mp_to=None):
        target = {}
        if dp_to is not None:
            target["dp"] = dp_to
        if mp_to is not None:
            target["mp"] = mp_to
        return pltpu.make_async_remote_copy(
            src_ref=src, dst_ref=dst, send_sem=send, recv_sem=recv,
            device_id=target, device_id_type=MESH,
        )

    kv_col = pl.multiple_of((mp * heads // GROUP) * HD, HD)
    loads = [
        pltpu.make_async_copy(
            src.at[:, pl.ds(kv_col, HD)], kv.at[i, pl.ds(first_row, rows), :], load_sems.at[i]
        )
        for i, src in enumerate((k_hbm, v_hbm))
    ]
    for copy in loads:
        copy.start()

    def w_load(d):
        block = jnp.where(left_half, d, n_mp - 1 - d)
        columns = pl.ds(pl.multiple_of(block * out_cols + slot * quarter, quarter), quarter)
        return pltpu.make_async_copy(w_hbm.at[:, columns], w.at[d], w_sems.at[d])

    for d in range(n_mp - 1, -1, -1):
        w_load(d).start()

    barrier = pltpu.get_barrier_semaphore()
    for r in range(1, chips):
        peer = ((chip + r) % chips) * 2 + core
        pl.semaphore_signal(barrier, inc=1, device_id={"dp": peer}, device_id_type=MESH)
    pl.semaphore_signal(barrier, inc=1, device_id={"dp": partner}, device_id_type=MESH)
    pl.semaphore_signal(barrier, inc=1, device_id={"dp": x_other}, device_id_type=MESH)

    @pl.when(mp > 0)
    def _():
        pl.semaphore_signal(barrier, inc=1, device_id={"mp": mp - 1}, device_id_type=MESH)

    @pl.when(mp < n_mp - 1)
    def _():
        pl.semaphore_signal(barrier, inc=1, device_id={"mp": mp + 1}, device_id_type=MESH)

    for copy in loads:
        copy.wait()
    pl.semaphore_wait(barrier, chips + 3 - jnp.where(is_end, 1, 0))

    def kv_copy(block, send_sem, recv_sem, target):
        part = kv.at[:, pl.ds(pl.multiple_of(block * rows, rows), rows), :]
        return remote(part, part, send_sem, recv_sem, target)

    sends = [
        kv_copy(dp, kv_send.at[r], kv_recv.at[r], ((chip + r) % chips) * 2 + core)
        for r in range(1, chips)
    ]
    sends.append(kv_copy(dp, pass_send.at[0], pass_recv.at[0], partner))
    for copy in sends:
        copy.start()

    def w_z(j):
        d = n_mp - 1 - j // w_chunks
        at = pl.ds(pl.multiple_of(y * (depth // 2) + j % w_chunks * chunk, chunk), chunk)
        return remote(
            w.at[d, at, :], w_end.at[d, at, :], wz_send.at[j], wz_recv.at[j], mp_to=mid_mp
        )

    def w_y(j, part):
        d = n_mp - 1 - j // w_chunks
        at = pl.ds(pl.multiple_of(part * (depth // 2) + j % w_chunks * chunk, chunk), chunk)
        return remote(
            w_end.at[d, at, :], w_end.at[d, at, :], wy_send.at[j], wy_recv.at[j], y_same
        )

    def pass_w(j):
        w_z(j).wait_recv()
        w_y(j, y).start()

    w_load(n_mp - 1).wait()

    @pl.when(is_end)
    def _():
        for j in range(w_chunks):
            w_z(j).start()

    own_segs = seg_ref[:, pl.ds(first_row, rows)].astype(jnp.float32)
    diagonal = lax.broadcasted_iota(jnp.int32, (rows, rows), 0) == lax.broadcasted_iota(
        jnp.int32, (rows, rows), 1
    )
    query_segs = jnp.sum(
        jnp.where(diagonal, jnp.broadcast_to(own_segs, (rows, rows)), 0.0), axis=1, keepdims=True
    )
    for start in range(0, tokens, key_span):
        key_segs = seg_ref[:, start : start + key_span].astype(jnp.float32)
        key_pos = start + lax.broadcasted_iota(jnp.int32, (rows, key_span), 1)
        query_pos = first_row + lax.broadcasted_iota(jnp.int32, (rows, key_span), 0)
        allowed = (query_segs == key_segs) & (key_pos <= query_pos)
        bias[:, start : start + key_span] = jnp.where(allowed, 0.0, -1e30)

    for r in range(1, chips):
        source = ((chip + chips - r) % chips) * 2 + core
        kv_copy(source, kv_send.at[r], kv_recv.at[r], dp).wait_recv()
        forward = kv_copy(source, pass_send.at[r], pass_recv.at[r], partner)
        forward.start()
        sends.append(forward)
    for r in range(chips):
        source = ((chip + chips - r) % chips) * 2 + 1 - core
        kv_copy(source, pass_send.at[r], pass_recv.at[r], dp).wait_recv()

    scale = math.log2(math.e) / math.sqrt(HD)

    def one_head(h, carry):
        columns = pl.ds(pl.multiple_of(h * HD, HD), HD)
        q = q_ref[:, columns]
        top = total = acc = None
        for start in range(0, tokens, key_span):
            span = slice(start, start + key_span)
            scores = lax.dot_general(
                q, kv[0, span, :], (((1,), (1,)), ((), ())), preferred_element_type=jnp.float32
            )
            scores = scores * scale + bias[:, span]
            new_top = jnp.max(scores, axis=1, keepdims=True)
            if top is not None:
                new_top = jnp.maximum(top, new_top)
            probs = jnp.exp2(scores - new_top)
            part_sum = jnp.sum(probs, axis=1, keepdims=True)
            part = jnp.dot(
                probs.astype(jnp.bfloat16), kv[1, span, :], preferred_element_type=jnp.float32
            )
            if top is None:
                total, acc = part_sum, part
            else:
                fade = jnp.exp2(top - new_top)
                total, acc = total * fade + part_sum, acc * fade + part
            top = new_top
        att[0, slot, :, columns] = (acc / total).astype(jnp.bfloat16)

        @pl.when(is_mid & (h % 2 == 1))
        def _():
            pass_w(h // 2)

        return carry

    lax.fori_loop(0, heads, one_head, 0)

    def rows_at(r):
        return pl.ds(pl.multiple_of(r * piece, piece), piece)

    def a_z(r):
        return remote(
            att.at[0, slot, rows_at(r), :], att.at[1, slot, rows_at(r), :],
            az_send.at[r], az_recv.at[r], mp_to=mid_mp,
        )

    def a_own(s, r, at):
        part = att.at[s, at, rows_at(r), :]
        k = s * r_count + r
        return remote(part, part, own_send.at[k], own_recv.at[k], partner)

    def a_x(s, r, at):
        part = att.at[s, at, rows_at(r), :]
        k = s * r_count + r
        return remote(part, part, ax_send.at[k], ax_recv.at[k], x_same)

    def a_rel(s, r, at):
        part = att.at[s, at, rows_at(r), :]
        k = s * r_count + r
        return remote(part, part, rel_send.at[k], rel_recv.at[k], partner)

    def pass_a(s, r):
        a_x(s, r, slot_x).wait_recv()
        a_rel(s, r, slot_x).start()

    def lhs(s, g, r):
        pair = jnp.where(g == 0, x, 1 - x) * 2
        return att[s, pl.ds(pair, 2), rows_at(r), :].reshape(2 * piece, depth)

    def product(s, g, r, d):
        weight = w if s == 0 else w_end
        return jnp.dot(lhs(s, g, r), weight[d], preferred_element_type=jnp.float32)

    def far(i):
        return remote(far_out.at[i], far_in.at[i], far_send.at[i], far_recv.at[i], mp_to=far_mp)

    def to_end(i):
        return remote(end_out.at[i], end_in.at[i], end_send.at[i], end_recv.at[i], mp_to=end_mp)

    def fin_copy(k, src, r, at, target):
        columns = pl.ds(pl.multiple_of(at * quarter, quarter), quarter)
        return remote(
            src, out_ref.at[rows_at(r), columns], fin_send.at[k * r_count + r],
            fin_recv.at[k * r_count + r], target,
        )

    def fin_copies(g, r):
        at = done.at[g, r]
        if g == 0:
            return [fin_copy(0, at.at[1 - core], r, slot, partner)]
        return [
            fin_copy(1, at.at[core], r, slot, x_same),
            fin_copy(2, at.at[1 - core], r, slot, x_other),
        ]

    def finish(g, r, value):
        done[g, r] = value.astype(jnp.bfloat16).reshape(2, piece, quarter)

        @pl.when(g == 0)
        def _():
            columns = pl.ds(pl.multiple_of(slot * quarter, quarter), quarter)
            out_ref[rows_at(r), columns] = done[0, r, core]
            for copy in fin_copies(0, r):
                copy.start()

        @pl.when(g == 1)
        def _():
            for copy in fin_copies(1, r):
                copy.start()

    for d in range(n_mp - 1):
        w_load(d).wait()

    def each(count, body):
        def run(i, carry):
            body(i)
            return carry

        lax.fori_loop(0, count, run, 0)

    def share_own(r):
        a_own(0, r, slot).start()
        a_x(0, r, slot).start()

    each(r_count, share_own)

    @pl.when(is_end)
    def _():
        each(r_count, lambda r: a_z(r).start())
        each(r_count, lambda r: a_z(r).wait_send())
        each(2 * w_chunks, lambda j: w_z(w_chunks + j).start())
        each(r_count, lambda r: pass_a(0, r))

        def ready(r):
            a_own(0, r, slot_partner).wait_recv()
            a_rel(0, r, slot_xo).wait_recv()

        each(r_count, ready)

        def last(i):
            g, r = i // r_count, i % r_count
            value = product(0, g, r, 0)
            to_end(i).wait_recv()
            finish(g, r, value + end_in[i].astype(jnp.float32))

        each(half_items, last)
        each(half_items // 2, lambda i: None)
        each((n_mp - 1) * w_chunks, lambda j: w_z(j).wait_send())

    @pl.when(is_mid)
    def _():
        def last(f):
            g, r = 1 - f // r_count, f % r_count
            value = product(0, g, r, 1) + product(1, g, r, 1)
            far(half_items + f).wait_recv()
            finish(g, r, value + far_in[half_items + f].astype(jnp.float32))

        def step(i):
            second = i // half_items
            j = i % half_items
            g = jnp.where(second == 0, j // r_count, 1 - j // r_count)
            r = i % r_count

            @pl.when(i < r_count)
            def _():
                a_z(r).wait_recv()
                a_own(1, r, slot).start()
                a_x(1, r, slot).start()
                a_own(0, r, slot_partner).wait_recv()
                a_own(1, r, slot_partner).wait_recv()

            @pl.when((i >= r_count) & (i < 2 * r_count))
            def _():
                a_rel(0, r, slot_xo).wait_recv()
                a_rel(1, r, slot_xo).wait_recv()

            @pl.when(j == 0)
            def _():
                each(w_chunks, lambda k: w_y(second * w_chunks + k, 1 - y).wait_recv())

            d = n_mp - 1 - second
            far_out[i] = (product(0, g, r, d) + product(1, g, r, d)).astype(jnp.bfloat16)
            far(i).start()

            @pl.when(i < r_count)
            def _():
                pass_a(0, r)

            @pl.when((i >= r_count - 1) & (i < 2 * r_count - 1))
            def _():
                pass_a(1, i - (r_count - 1))

            @pl.when((i >= w_chunks) & (i < 3 * w_chunks))
            def _():
                pass_w(i)

            @pl.when((i >= 1) & (i <= half_items))
            def _():
                k = i - 1
                value = product(0, k // r_count, k % r_count, 0)
                far(k).wait_recv()
                end_out[k] = (value + far_in[k].astype(jnp.float32)).astype(jnp.bfloat16)
                to_end(k).start()

            @pl.when(i >= half_items + half_items // 2)
            def _():
                @pl.when(i == half_items + half_items // 2)
                def _():
                    each(w_chunks, lambda k: w_y(2 * w_chunks + k, 1 - y).wait_recv())

                f = 2 * (i - half_items - half_items // 2)
                each(2, lambda k: last(f + k))

        each(2 * half_items, step)

        each((n_mp - 1) * w_chunks, lambda j: w_y(j, y).wait_send())
        each(2 * half_items, lambda i: far(i).wait_send())
        each(half_items, lambda i: to_end(i).wait_send())

        def drain(r):
            a_own(1, r, slot).wait_send()
            a_x(1, r, slot).wait_send()
            a_rel(1, r, slot_x).wait_send()

        each(r_count, drain)

    for copy in sends:
        copy.wait_send()

    def drain(r):
        a_own(0, r, slot).wait_send()
        a_x(0, r, slot).wait_send()
        a_rel(0, r, slot_x).wait_send()
        for copy in fin_copies(0, r) + fin_copies(1, r):
            copy.wait_send()
        fin_copy(0, done.at[0, r, 0], r, slot_partner, partner).wait_recv()
        fin_copy(1, done.at[0, r, 0], r, slot_x, x_same).wait_recv()
        fin_copy(2, done.at[0, r, 0], r, slot_xo, x_other).wait_recv()

    each(r_count, drain)


def pair_call(n_dp, n_mp, segment_ids, queries, keys, values, out_weight):
    rows, tokens = queries.shape[0], segment_ids.shape[0]
    depth, width = out_weight.shape
    out_cols = width // n_mp
    quarter = out_cols // 4
    piece = rows // 4
    items = 2 * (rows // piece)
    key_span = min(2048, tokens)
    dma = pltpu.SemaphoreType.DMA
    vmem = pl.BlockSpec(memory_space=pltpu.VMEM)
    hbm = pl.BlockSpec(memory_space=pl.ANY)

    def buffer(*shape):
        return pltpu.VMEM(shape, jnp.bfloat16)

    return pl.pallas_call(
        functools.partial(pair_kernel, n_dp, n_mp, key_span, piece),
        out_shape=jax.ShapeDtypeStruct((rows, out_cols), jnp.bfloat16),
        in_specs=[vmem, vmem, hbm, hbm, hbm],
        out_specs=vmem,
        scratch_shapes=[
            buffer(2, tokens, HD),
            buffer(n_mp, depth, quarter),
            buffer(n_mp, depth, quarter),
            pltpu.VMEM((rows, tokens), jnp.float32),
            buffer(2, 4, rows, depth),
            buffer(2 * items, 2 * piece, quarter), buffer(2 * items, 2 * piece, quarter),
            buffer(items, 2 * piece, quarter), buffer(items, 2 * piece, quarter),
            buffer(2, rows // piece, 2, piece, quarter),
            dma((2,)), dma((n_mp,)),
            dma((4,)), dma((4,)), dma((4,)), dma((4,)),
            dma((12,)), dma((12,)), dma((12,)), dma((12,)), dma((4,)), dma((4,)),
            dma((8,)), dma((8,)), dma((8,)), dma((8,)), dma((8,)), dma((8,)),
            dma((2 * items,)), dma((2 * items,)), dma((items,)), dma((items,)),
            dma((12,)), dma((12,)),
        ],
        compiler_params=pltpu.CompilerParams(
            collective_id=1, has_side_effects=True, vmem_limit_bytes=60 * 1024 * 1024
        ),
    )(segment_ids.reshape(1, tokens), queries, keys, values, out_weight)


def relay_kernel(
    n_dp, n_mp, key_span, chunk,
    seg_ref, q_ref, k_hbm, v_hbm, w_hbm, out_ref,
    kv, w, bias, attended, from_left, from_right, to_right, to_left,
    load_sems, w_sem, kv_send, kv_recv, pass_send, pass_recv,
    right_send, right_recv, left_send, left_recv,
):
    rows = q_ref.shape[0]
    heads = q_ref.shape[1] // HD
    tokens = n_dp * rows
    out_cols = out_ref.shape[1]
    pieces = out_cols // chunk
    chips = n_dp // 2
    dp, mp = lax.axis_index("dp"), lax.axis_index("mp")
    core, chip = dp % 2, dp // 2
    partner = dp + 1 - 2 * core
    first_row = pl.multiple_of(dp * rows, rows)

    kv_col = pl.multiple_of((mp * heads // GROUP) * HD, HD)
    own = kv.at[:, pl.ds(first_row, rows), :]
    loads = [
        pltpu.make_async_copy(
            src.at[:, pl.ds(kv_col, HD)], kv.at[i, pl.ds(first_row, rows), :], load_sems.at[i]
        )
        for i, src in enumerate((k_hbm, v_hbm))
    ]
    for copy in loads:
        copy.start()
    w_copy = pltpu.make_async_copy(w_hbm, w, w_sem)
    w_copy.start()

    barrier = pltpu.get_barrier_semaphore()
    for r in range(1, chips):
        peer = ((chip + r) % chips) * 2 + core
        pl.semaphore_signal(barrier, inc=1, device_id={"dp": peer}, device_id_type=MESH)
    pl.semaphore_signal(barrier, inc=1, device_id={"dp": partner}, device_id_type=MESH)

    @pl.when(mp > 0)
    def _():
        pl.semaphore_signal(barrier, inc=1, device_id={"mp": mp - 1}, device_id_type=MESH)

    @pl.when(mp < n_mp - 1)
    def _():
        pl.semaphore_signal(barrier, inc=1, device_id={"mp": mp + 1}, device_id_type=MESH)

    ends = jnp.where(mp == 0, 1, 0) + jnp.where(mp == n_mp - 1, 1, 0)
    for copy in loads:
        copy.wait()
    pl.semaphore_wait(barrier, chips + 2 - ends)

    def kv_copy(block, send_sem, recv_sem, target):
        part = kv.at[:, pl.ds(pl.multiple_of(block * rows, rows), rows), :]
        return pltpu.make_async_remote_copy(
            src_ref=part, dst_ref=part, send_sem=send_sem, recv_sem=recv_sem,
            device_id={"dp": target}, device_id_type=MESH,
        )

    sends = [
        kv_copy(dp, kv_send.at[r], kv_recv.at[r], ((chip + r) % chips) * 2 + core)
        for r in range(1, chips)
    ]
    sends.append(kv_copy(dp, pass_send.at[0], pass_recv.at[0], partner))
    for copy in sends:
        copy.start()

    own_segs = seg_ref[:, pl.ds(first_row, rows)].astype(jnp.float32)
    diagonal = lax.broadcasted_iota(jnp.int32, (rows, rows), 0) == lax.broadcasted_iota(
        jnp.int32, (rows, rows), 1
    )
    query_segs = jnp.sum(
        jnp.where(diagonal, jnp.broadcast_to(own_segs, (rows, rows)), 0.0), axis=1, keepdims=True
    )
    for start in range(0, tokens, key_span):
        key_segs = seg_ref[:, start : start + key_span].astype(jnp.float32)
        key_pos = start + lax.broadcasted_iota(jnp.int32, (rows, key_span), 1)
        query_pos = first_row + lax.broadcasted_iota(jnp.int32, (rows, key_span), 0)
        allowed = (query_segs == key_segs) & (key_pos <= query_pos)
        bias[:, start : start + key_span] = jnp.where(allowed, 0.0, -1e30)

    for r in range(1, chips):
        source = ((chip + chips - r) % chips) * 2 + core
        kv_copy(source, kv_send.at[r], kv_recv.at[r], dp).wait_recv()
        forward = kv_copy(source, pass_send.at[r], pass_recv.at[r], partner)
        forward.start()
        sends.append(forward)
    for r in range(chips):
        source = ((chip + chips - r) % chips) * 2 + 1 - core
        kv_copy(source, pass_send.at[r], pass_recv.at[r], dp).wait_recv()

    scale = math.log2(math.e) / math.sqrt(HD)

    def one_head(h, carry):
        columns = pl.ds(pl.multiple_of(h * HD, HD), HD)
        q = q_ref[:, columns]
        top = total = acc = None
        for start in range(0, tokens, key_span):
            span = slice(start, start + key_span)
            scores = lax.dot_general(
                q, kv[0, span, :], (((1,), (1,)), ((), ())), preferred_element_type=jnp.float32
            )
            scores = scores * scale + bias[:, span]
            new_top = jnp.max(scores, axis=1, keepdims=True)
            if top is not None:
                new_top = jnp.maximum(top, new_top)
            probs = jnp.exp2(scores - new_top)
            part_sum = jnp.sum(probs, axis=1, keepdims=True)
            part = jnp.dot(
                probs.astype(jnp.bfloat16), kv[1, span, :], preferred_element_type=jnp.float32
            )
            if top is None:
                total, acc = part_sum, part
            else:
                fade = jnp.exp2(top - new_top)
                total, acc = total * fade + part_sum, acc * fade + part
            top = new_top
        attended[:, columns] = (acc / total).astype(jnp.bfloat16)
        return carry

    lax.fori_loop(0, heads, one_head, 0)
    w_copy.wait()

    def project(d, k):
        columns = pl.ds(pl.multiple_of(d * out_cols + k * chunk, chunk), chunk)
        return jnp.dot(attended[...], w[:, columns], preferred_element_type=jnp.float32)

    def right_copy(d, k):
        at = d * pieces + k
        return pltpu.make_async_remote_copy(
            src_ref=to_right.at[at], dst_ref=from_left.at[at],
            send_sem=right_send.at[at], recv_sem=right_recv.at[at],
            device_id={"mp": mp + 1}, device_id_type=MESH,
        )

    def left_copy(d, k):
        at = d * pieces + k
        return pltpu.make_async_remote_copy(
            src_ref=to_left.at[at], dst_ref=from_right.at[at],
            send_sem=left_send.at[at], recv_sem=left_recv.at[at],
            device_id={"mp": mp - 1}, device_id_type=MESH,
        )

    def relay(d, k, copy_of, staged, arrived, at_end):
        at = d * pieces + k
        value = project(d, k)

        @pl.when(at_end)
        def _():
            staged[at] = value.astype(jnp.bfloat16)

        @pl.when(jnp.logical_not(at_end))
        def _():
            copy_of(d, k).wait_recv()
            staged[at] = (value + arrived[at].astype(jnp.float32)).astype(jnp.bfloat16)

        copy_of(d, k).start()

    items = (n_mp - 1) * pieces

    def step(t, carry):
        right_item = t - LAG * mp
        left_item = t - LAG * (n_mp - 1 - mp)
        right_at = jnp.maximum(right_item, 0)
        left_at = jnp.maximum(left_item, 0)
        right_to = n_mp - 1 - right_at // pieces
        left_to = left_at // pieces

        @pl.when((right_item >= 0) & (right_item < items) & (right_to > mp))
        def _():
            relay(right_to, right_at % pieces, right_copy, to_right, from_left, mp == 0)

        @pl.when((left_item >= 0) & (left_item < items) & (left_to < mp))
        def _():
            relay(left_to, left_at % pieces, left_copy, to_left, from_right, mp == n_mp - 1)

        return carry

    lax.fori_loop(0, items + LAG * (n_mp - 1), step, 0)

    def finish(k, carry):
        at = mp * pieces + k
        columns = pl.ds(pl.multiple_of(k * chunk, chunk), chunk)
        value = project(mp, k)

        @pl.when(mp == 0)
        def _():
            left_copy(mp, k).wait_recv()
            out_ref[:, columns] = (value + from_right[at].astype(jnp.float32)).astype(jnp.bfloat16)

        @pl.when(mp == n_mp - 1)
        def _():
            right_copy(mp, k).wait_recv()
            out_ref[:, columns] = (value + from_left[at].astype(jnp.float32)).astype(jnp.bfloat16)

        @pl.when((mp > 0) & (mp < n_mp - 1))
        def _():
            left_copy(mp, k).wait_recv()
            right_copy(mp, k).wait_recv()
            both = from_left[at].astype(jnp.float32) + from_right[at].astype(jnp.float32)
            out_ref[:, columns] = (value + both).astype(jnp.bfloat16)

        return carry

    lax.fori_loop(0, pieces, finish, 0)

    for copy in sends:
        copy.wait_send()

    def drain(i, carry):
        s, k = i // pieces, i % pieces

        @pl.when(n_mp - 1 - s > mp)
        def _():
            right_copy(n_mp - 1 - s, k).wait_send()

        @pl.when(s < mp)
        def _():
            left_copy(s, k).wait_send()

        return carry

    lax.fori_loop(0, (n_mp - 1) * pieces, drain, 0)


def relay_call(n_dp, n_mp, segment_ids, queries, keys, values, out_weight):
    rows, tokens = queries.shape[0], segment_ids.shape[0]
    depth, width = out_weight.shape
    out_cols = width // n_mp
    chunk = min(256, out_cols)
    slots = n_mp * (out_cols // chunk)
    key_span = min(2048, tokens)
    dma = pltpu.SemaphoreType.DMA
    vmem = pl.BlockSpec(memory_space=pltpu.VMEM)
    hbm = pl.BlockSpec(memory_space=pl.ANY)
    stage = pltpu.VMEM((slots, rows, chunk), jnp.bfloat16)
    return pl.pallas_call(
        functools.partial(relay_kernel, n_dp, n_mp, key_span, chunk),
        out_shape=jax.ShapeDtypeStruct((rows, out_cols), jnp.bfloat16),
        in_specs=[vmem, vmem, hbm, hbm, hbm],
        out_specs=vmem,
        scratch_shapes=[
            pltpu.VMEM((2, tokens, HD), jnp.bfloat16),
            pltpu.VMEM((depth, width), jnp.bfloat16),
            pltpu.VMEM((rows, tokens), jnp.float32),
            pltpu.VMEM((rows, queries.shape[1]), jnp.bfloat16),
            stage, stage, stage, stage,
            dma((2,)), dma,
            dma((n_dp // 2,)), dma((n_dp // 2,)), dma((n_dp // 2,)), dma((n_dp // 2,)),
            dma((slots,)), dma((slots,)), dma((slots,)), dma((slots,)),
        ],
        compiler_params=pltpu.CompilerParams(
            collective_id=0, has_side_effects=True, vmem_limit_bytes=60 * 1024 * 1024
        ),
    )(segment_ids.reshape(1, tokens), queries, keys, values, out_weight)


def solution(mesh):
    n_dp, n_mp = mesh.shape["dp"], mesh.shape["mp"]
    call = pair_call if (n_dp, n_mp) == (8, 4) else relay_call
    on_device = functools.partial(call, n_dp, n_mp)

    return jax.shard_map(
        on_device,
        mesh=mesh,
        in_specs=(P(), P("dp", "mp"), P("dp", None), P("dp", None), P("mp", None)),
        out_specs=P("dp", "mp"),
        check_vma=False,
    )
```

```python
import functools
import math

import jax
import jax.numpy as jnp
from jax import lax
from jax.experimental import pallas as pl
from jax.experimental.pallas import tpu as pltpu
from jax.sharding import PartitionSpec as P

HD = 128
GROUP = 8
LAG = 2
PARTS = 4
MESH = pl.DeviceIdType.MESH


def pair_kernel(
    n_dp, n_mp, key_span, piece,
    seg_ref, q_ref, k_hbm, v_hbm, w_hbm, out_ref,
    kv, w, w_end, bias, att, far_out, far_in, end_out, end_in, done,
    load_sems, w_sems, kv_send, kv_recv, pass_send, pass_recv,
    wz_send, wz_recv, wy_send, wy_recv, az_send, az_recv,
    own_send, own_recv, ax_send, ax_recv, rel_send, rel_recv,
    far_send, far_recv, end_send, end_recv, fin_send, fin_recv, keep_sems,
):
    rows = q_ref.shape[0]
    heads = q_ref.shape[1] // HD
    tokens = n_dp * rows
    out_cols = out_ref.shape[1]
    depth, quarter = w.shape[1], w.shape[2]
    r_count = rows // piece
    half_items = 2 * r_count
    w_chunks = 4
    chunk = depth // 2 // w_chunks
    dp, mp = lax.axis_index("dp"), lax.axis_index("mp")
    core, chip = dp % 2, dp // 2
    x, y = chip % 2, chip // 2
    partner = dp + 1 - 2 * core
    x_same, x_other = (y * 2 + 1 - x) * 2 + core, (y * 2 + 1 - x) * 2 + 1 - core
    y_same = ((1 - y) * 2 + x) * 2 + core
    first_row = pl.multiple_of(dp * rows, rows)
    left_half = mp < n_mp // 2
    is_end = (mp == 0) | (mp == n_mp - 1)
    is_mid = jnp.logical_not(is_end)
    end_mp = jnp.where(left_half, 0, n_mp - 1)
    mid_mp = jnp.where(left_half, 1, n_mp - 2)
    far_mp = n_mp - 1 - mp
    slot, slot_partner = x * 2 + core, x * 2 + 1 - core
    slot_x, slot_xo = (1 - x) * 2 + core, (1 - x) * 2 + 1 - core

    def remote(src, dst, send, recv, dp_to=None, mp_to=None):
        target = {}
        if dp_to is not None:
            target["dp"] = dp_to
        if mp_to is not None:
            target["mp"] = mp_to
        return pltpu.make_async_remote_copy(
            src_ref=src, dst_ref=dst, send_sem=send, recv_sem=recv,
            device_id=target, device_id_type=MESH,
        )

    kv_col = pl.multiple_of((mp * heads // GROUP) * HD, HD)
    loads = [
        pltpu.make_async_copy(
            src.at[:, pl.ds(kv_col, HD)], kv.at[i, pl.ds(first_row, rows), :], load_sems.at[i]
        )
        for i, src in enumerate((k_hbm, v_hbm))
    ]
    for copy in loads:
        copy.start()

    def w_load(d):
        block = jnp.where(left_half, d, n_mp - 1 - d)
        columns = pl.ds(pl.multiple_of(block * out_cols + slot * quarter, quarter), quarter)
        return pltpu.make_async_copy(w_hbm.at[:, columns], w.at[d], w_sems.at[d])

    for d in range(n_mp - 1, -1, -1):
        w_load(d).start()

    barrier = pltpu.get_barrier_semaphore()
    for peer in (partner, x_same, x_other, y_same):
        pl.semaphore_signal(barrier, inc=1, device_id={"dp": peer}, device_id_type=MESH)

    @pl.when(mp > 0)
    def _():
        pl.semaphore_signal(barrier, inc=1, device_id={"mp": mp - 1}, device_id_type=MESH)

    @pl.when(mp < n_mp - 1)
    def _():
        pl.semaphore_signal(barrier, inc=1, device_id={"mp": mp + 1}, device_id_type=MESH)

    for copy in loads:
        copy.wait()
    pl.semaphore_wait(barrier, 6 - jnp.where(is_end, 1, 0))

    OWN, FROM_X, FROM_Y, FROM_XY = range(4)

    def kv_copy(block, k, target, sems):
        part = kv.at[:, pl.ds(pl.multiple_of(block * rows, rows), rows), :]
        return remote(part, part, sems[0].at[k], sems[1].at[k], target)

    links, passes = (kv_send, kv_recv), (pass_send, pass_recv)
    xy_same = ((1 - y) * 2 + 1 - x) * 2 + core
    blocks = (dp, x_same, y_same, xy_same)

    def across(block):
        return block + 1 - 2 * core

    kv_copy(dp, FROM_X, x_same, links).start()
    kv_copy(dp, OWN, partner, passes).start()

    @pl.when(y == 0)
    def _():
        kv_copy(dp, FROM_Y, y_same, links).start()

    def w_z(j):
        d = n_mp - 1 - j // w_chunks
        at = pl.ds(pl.multiple_of(y * (depth // 2) + j % w_chunks * chunk, chunk), chunk)
        return remote(
            w.at[d, at, :], w_end.at[d, at, :], wz_send.at[j], wz_recv.at[j], mp_to=mid_mp
        )

    def w_y(j, side, part=None):
        d = n_mp - 1 - j // w_chunks
        count = chunk if part is None else chunk // PARTS
        start = side * (depth // 2) + j % w_chunks * chunk + (0 if part is None else part * count)
        at = pl.ds(pl.multiple_of(start, count), count)
        return remote(
            w_end.at[d, at, :], w_end.at[d, at, :], wy_send.at[j], wy_recv.at[j], y_same
        )

    def pass_w(j):
        w_z(j).wait_recv()
        for part in range(PARTS):
            w_y(j, y, part).start()

    w_load(n_mp - 1).wait()

    @pl.when(is_end)
    def _():
        for j in range(w_chunks):
            w_z(j).start()

    own_segs = seg_ref[:, pl.ds(first_row, rows)].astype(jnp.float32)
    diagonal = lax.broadcasted_iota(jnp.int32, (rows, rows), 0) == lax.broadcasted_iota(
        jnp.int32, (rows, rows), 1
    )
    query_segs = jnp.sum(
        jnp.where(diagonal, jnp.broadcast_to(own_segs, (rows, rows)), 0.0), axis=1, keepdims=True
    )
    for start in range(0, tokens, key_span):
        key_segs = seg_ref[:, start : start + key_span].astype(jnp.float32)
        key_pos = start + lax.broadcasted_iota(jnp.int32, (rows, key_span), 1)
        query_pos = first_row + lax.broadcasted_iota(jnp.int32, (rows, key_span), 0)
        allowed = (query_segs == key_segs) & (key_pos <= query_pos)
        bias[:, start : start + key_span] = jnp.where(allowed, 0.0, -1e30)

    def rows_at(r):
        return pl.ds(pl.multiple_of(r * piece, piece), piece)

    def a_z(r):
        return remote(
            att.at[0, slot, rows_at(r), :], att.at[1, slot, rows_at(r), :],
            az_send.at[r], az_recv.at[r], mp_to=mid_mp,
        )

    def a_own(s, r, at, part=None):
        count = piece if part is None else piece // PARTS
        start = r * piece + (0 if part is None else part * count)
        part = att.at[s, at, pl.ds(pl.multiple_of(start, count), count), :]
        k = s * r_count + r
        return remote(part, part, own_send.at[k], own_recv.at[k], partner)

    def a_rel(s, r, at, part=None):
        count = piece if part is None else piece // PARTS
        start = r * piece + (0 if part is None else part * count)
        part = att.at[s, at, pl.ds(pl.multiple_of(start, count), count), :]
        k = s * r_count + r
        return remote(part, part, rel_send.at[k], rel_recv.at[k], partner)

    def in_parts(copy, s, r, at):
        for part in range(PARTS):
            copy(s, r, at, part).start()

    def a_x(s, r, at):
        part = att.at[s, at, rows_at(r), :]
        k = s * r_count + r
        return remote(part, part, ax_send.at[k], ax_recv.at[k], x_same)

    def pass_a(s, r):
        a_x(s, r, slot_x).wait_recv()
        in_parts(a_rel, s, r, slot_x)

    def lhs(s, g, r):
        pair = jnp.where(g == 0, x, 1 - x) * 2
        return att[s, pl.ds(pair, 2), rows_at(r), :].reshape(2 * piece, depth)

    def product(s, g, r, d):
        weight = w if s == 0 else w_end
        return jnp.dot(lhs(s, g, r), weight[d], preferred_element_type=jnp.float32)

    def far(i):
        return remote(far_out.at[i], far_in.at[i], far_send.at[i], far_recv.at[i], mp_to=far_mp)

    def to_end(i):
        return remote(end_out.at[i], end_in.at[i], end_send.at[i], end_recv.at[i], mp_to=end_mp)

    def fin_copy(k, src, r, at, target):
        columns = pl.ds(pl.multiple_of(at * quarter, quarter), quarter)
        return remote(
            src, out_ref.at[rows_at(r), columns], fin_send.at[k * r_count + r],
            fin_recv.at[k * r_count + r], target,
        )

    def fin_copies(g, r):
        at = done.at[g, r]
        if g == 0:
            return [fin_copy(0, at.at[1 - core], r, slot, partner)]
        return [
            fin_copy(1, at.at[core], r, slot, x_same),
            fin_copy(2, at.at[1 - core], r, slot, x_other),
        ]

    def keep(r):
        columns = pl.ds(pl.multiple_of(slot * quarter, quarter), quarter)
        return pltpu.make_async_copy(
            done.at[0, r, core], out_ref.at[rows_at(r), columns], keep_sems.at[r]
        )

    def finish(g, r, value):
        done[g, r] = value.astype(jnp.bfloat16).reshape(2, piece, quarter)

        @pl.when(g == 0)
        def _():
            keep(r).start()
            for copy in fin_copies(0, r):
                copy.start()

        @pl.when(g == 1)
        def _():
            for copy in fin_copies(1, r):
                copy.start()

    def each(count, body):
        def run(i, carry):
            body(i)
            return carry

        lax.fori_loop(0, count, run, 0)

    @pl.when(y == 1)
    def _():
        kv_copy(y_same, FROM_Y, dp, links).wait_recv()
        kv_copy(y_same, FROM_XY, x_same, links).start()
        kv_copy(y_same, FROM_Y, partner, passes).start()

    kv_copy(x_same, FROM_X, dp, links).wait_recv()
    kv_copy(x_same, FROM_X, partner, passes).start()

    @pl.when(is_mid)
    def _():
        pass_w(0)

    @pl.when(y == 1)
    def _():
        kv_copy(xy_same, FROM_XY, dp, links).wait_recv()
        kv_copy(xy_same, FROM_XY, partner, passes).start()
        for k in (FROM_Y, FROM_XY):
            kv_copy(across(blocks[k]), k, dp, passes).wait_recv()

    for k in (OWN, FROM_X):
        kv_copy(across(blocks[k]), k, dp, passes).wait_recv()

    @pl.when(is_mid & (y == 1))
    def _():
        pass_w(1)

    scale = math.log2(math.e) / math.sqrt(HD)
    stack = heads
    span = 4 * rows

    def attend(r, starts):
        q = jnp.concatenate([q_ref[rows_at(r), k * HD : (k + 1) * HD] for k in range(stack)])
        top = total = acc = None
        for start in starts:
            keys = slice(start, start + span)
            scores = lax.dot_general(
                q, kv[0, keys, :], (((1,), (1,)), ((), ())), preferred_element_type=jnp.float32
            )
            scores = scores * scale + jnp.concatenate([bias[rows_at(r), keys]] * stack)
            new_top = jnp.max(scores, axis=1, keepdims=True)
            if top is not None:
                new_top = jnp.maximum(top, new_top)
            probs = jnp.exp2(scores - new_top)
            part_sum = jnp.sum(probs, axis=1, keepdims=True)
            part = jnp.dot(
                probs.astype(jnp.bfloat16), kv[1, keys, :], preferred_element_type=jnp.float32
            )
            if top is None:
                total, acc = part_sum, part
            else:
                fade = jnp.exp2(top - new_top)
                total, acc = total * fade + part_sum, acc * fade + part
            top = new_top
        out = (acc / total).astype(jnp.bfloat16)
        for k in range(stack):
            att[0, slot, rows_at(r), k * HD : (k + 1) * HD] = out[k * piece : (k + 1) * piece]

    def attend_piece(r):
        for pair, starts in ((0, (0,)), (1, (span, 0))):
            @pl.when(y == pair)
            def _():
                attend(r, starts)

        in_parts(a_own, 0, r, slot)

        @pl.when(is_end)
        def _():
            a_x(0, r, slot).start()
            a_z(r).start()

        @pl.when(is_mid & (r < 2))
        def _():
            a_x(0, r, slot).start()

        @pl.when(is_mid & (r == 3))
        def _():
            a_x(0, 2, slot).start()

        @pl.when(is_mid & (y == 1) & (r % 2 == 0))
        def _():
            pass_w(2 + r // 2)

        @pl.when(is_mid & (y == 0) & (r >= 1))
        def _():
            pass_w(r)

    each(r_count, attend_piece)

    for d in range(n_mp - 1):
        w_load(d).wait()

    def drain_early():
        for k in (OWN, FROM_X):
            kv_copy(blocks[k], k, partner, passes).wait_send()
        kv_copy(dp, FROM_X, x_same, links).wait_send()

        @pl.when(y == 0)
        def _():
            kv_copy(dp, FROM_Y, y_same, links).wait_send()

        @pl.when(y == 1)
        def _():
            kv_copy(y_same, FROM_XY, x_same, links).wait_send()
            for k in (FROM_Y, FROM_XY):
                kv_copy(blocks[k], k, partner, passes).wait_send()

        def sent(r):
            a_own(0, r, slot).wait_send()
            a_x(0, r, slot).wait_send()
            a_rel(0, r, slot_x).wait_send()

        each(r_count, sent)

    @pl.when(is_end)
    def _():
        each(r_count - 1, lambda r: a_z(r).wait_send())
        w_z(w_chunks).start()
        a_z(r_count - 1).wait_send()
        w_z(w_chunks + 1).start()

        def next_w(j):
            w_z(w_chunks + j).wait_send()
            w_z(w_chunks + j + 2).start()

        each(r_count, lambda r: pass_a(0, r))
        each(2 * w_chunks - 2, next_w)
        drain_early()

        def ready(r):
            a_own(0, r, slot_partner).wait_recv()
            a_rel(0, r, slot_xo).wait_recv()

        each(r_count, ready)

        def last(i):
            g, r = i // r_count, i % r_count
            value = product(0, g, r, 0)
            to_end(i).wait_recv()
            finish(g, r, value + end_in[i].astype(jnp.float32))

        each(half_items, last)
        each(w_chunks, lambda j: w_z(j).wait_send())
        each(2, lambda j: w_z(3 * w_chunks - 2 + j).wait_send())

    @pl.when(is_mid)
    def _():
        def last(f):
            g, r = 1 - f // r_count, f % r_count
            value = product(0, g, r, 1) + product(1, g, r, 1)
            far(half_items + f).wait_recv()
            finish(g, r, value + far_in[half_items + f].astype(jnp.float32))

        def step(i):
            second = i // half_items
            j = i % half_items
            g = jnp.where(second == 0, j // r_count, 1 - j // r_count)
            r = i % r_count

            @pl.when(i < r_count)
            def _():
                a_z(r).wait_recv()
                in_parts(a_own, 1, r, slot)
                a_own(0, r, slot_partner).wait_recv()
                a_own(1, r, slot_partner).wait_recv()

            @pl.when((i >= r_count) & (i < 2 * r_count))
            def _():
                a_rel(0, r, slot_xo).wait_recv()
                a_rel(1, r, slot_xo).wait_recv()

            @pl.when(j == 0)
            def _():
                each(w_chunks, lambda k: w_y(second * w_chunks + k, 1 - y).wait_recv())

            d = n_mp - 1 - second
            far_out[i] = (product(0, g, r, d) + product(1, g, r, d)).astype(jnp.bfloat16)
            far(i).start()

            @pl.when(i < r_count - 1)
            def _():
                a_x(1, r, slot).start()

            @pl.when(i == r_count - 1)
            def _():
                a_x(0, r_count - 1, slot).start()

            @pl.when(i == r_count)
            def _():
                a_x(1, r_count - 1, slot).start()

            @pl.when((i >= w_chunks - 1) & (i < 2 * w_chunks - 1))
            def _():
                pass_w(i + 1)

            @pl.when((i >= 2 * w_chunks) & (i < 3 * w_chunks))
            def _():
                pass_w(i)

            @pl.when((i >= LAG) & (i < half_items + LAG))
            def _():
                k = i - LAG
                value = product(0, k // r_count, k % r_count, 0)
                far(k).wait_recv()
                end_out[k] = (value + far_in[k].astype(jnp.float32)).astype(jnp.bfloat16)
                to_end(k).start()

            @pl.when(i < r_count - 1)
            def _():
                pass_a(0, r)

            @pl.when((i >= 2) & (i < r_count + 1))
            def _():
                pass_a(1, i - 2)

            @pl.when(i == r_count + 1)
            def _():
                pass_a(0, r_count - 1)

            @pl.when(i == r_count + 2)
            def _():
                pass_a(1, r_count - 1)

            @pl.when(i >= half_items + half_items // 2)
            def _():
                @pl.when(i == half_items + half_items // 2)
                def _():
                    each(w_chunks, lambda k: w_y(2 * w_chunks + k, 1 - y).wait_recv())

                @pl.when(i == 2 * half_items - 1)
                def _():
                    each((n_mp - 1) * w_chunks, lambda j: w_y(j, y).wait_send())
                    each(2 * half_items - 2, lambda k: far(k).wait_send())
                    each(half_items, lambda k: to_end(k).wait_send())

                    def sent(r):
                        a_own(1, r, slot).wait_send()
                        a_x(1, r, slot).wait_send()
                        a_rel(1, r, slot_x).wait_send()

                    each(r_count, sent)
                    drain_early()

                f = 2 * (i - half_items - half_items // 2)
                each(2, lambda k: last(f + k))

        each(2 * half_items, step)
        each(2, lambda k: far(2 * half_items - 2 + k).wait_send())

    def drain(r):
        keep(r).wait()
        for copy in fin_copies(0, r) + fin_copies(1, r):
            copy.wait_send()
        fin_copy(1, done.at[0, r, 0], r, slot_x, x_same).wait_recv()
        fin_copy(2, done.at[0, r, 0], r, slot_xo, x_other).wait_recv()
        fin_copy(0, done.at[0, r, 0], r, slot_partner, partner).wait_recv()

    each(r_count, drain)


def pair_call(n_dp, n_mp, segment_ids, queries, keys, values, out_weight):
    rows, tokens = queries.shape[0], segment_ids.shape[0]
    depth, width = out_weight.shape
    out_cols = width // n_mp
    quarter = out_cols // 4
    piece = rows // 4
    items = 2 * (rows // piece)
    key_span = min(2048, tokens)
    dma = pltpu.SemaphoreType.DMA
    vmem = pl.BlockSpec(memory_space=pltpu.VMEM)
    hbm = pl.BlockSpec(memory_space=pl.ANY)

    def buffer(*shape):
        return pltpu.VMEM(shape, jnp.bfloat16)

    return pl.pallas_call(
        functools.partial(pair_kernel, n_dp, n_mp, key_span, piece),
        out_shape=jax.ShapeDtypeStruct((rows, out_cols), jnp.bfloat16),
        in_specs=[vmem, vmem, hbm, hbm, hbm],
        out_specs=hbm,
        scratch_shapes=[
            buffer(2, tokens, HD),
            buffer(n_mp, depth, quarter),
            buffer(n_mp, depth, quarter),
            pltpu.VMEM((rows, tokens), jnp.float32),
            buffer(2, 4, rows, depth),
            buffer(2 * items, 2 * piece, quarter), buffer(2 * items, 2 * piece, quarter),
            buffer(items, 2 * piece, quarter), buffer(items, 2 * piece, quarter),
            buffer(2, rows // piece, 2, piece, quarter),
            dma((2,)), dma((n_mp,)),
            dma((4,)), dma((4,)), dma((4,)), dma((4,)),
            dma((12,)), dma((12,)), dma((12,)), dma((12,)), dma((4,)), dma((4,)),
            dma((8,)), dma((8,)), dma((8,)), dma((8,)), dma((8,)), dma((8,)),
            dma((2 * items,)), dma((2 * items,)), dma((items,)), dma((items,)),
            dma((12,)), dma((12,)), dma((4,)),
        ],
        compiler_params=pltpu.CompilerParams(
            collective_id=1, has_side_effects=True, vmem_limit_bytes=60 * 1024 * 1024
        ),
    )(segment_ids.reshape(1, tokens), queries, keys, values, out_weight)


def relay_kernel(
    n_dp, n_mp, key_span, chunk,
    seg_ref, q_ref, k_hbm, v_hbm, w_hbm, out_ref,
    kv, w, bias, attended, from_left, from_right, to_right, to_left,
    load_sems, w_sem, kv_send, kv_recv, pass_send, pass_recv,
    right_send, right_recv, left_send, left_recv,
):
    rows = q_ref.shape[0]
    heads = q_ref.shape[1] // HD
    tokens = n_dp * rows
    out_cols = out_ref.shape[1]
    pieces = out_cols // chunk
    chips = n_dp // 2
    dp, mp = lax.axis_index("dp"), lax.axis_index("mp")
    core, chip = dp % 2, dp // 2
    partner = dp + 1 - 2 * core
    first_row = pl.multiple_of(dp * rows, rows)

    kv_col = pl.multiple_of((mp * heads // GROUP) * HD, HD)
    own = kv.at[:, pl.ds(first_row, rows), :]
    loads = [
        pltpu.make_async_copy(
            src.at[:, pl.ds(kv_col, HD)], kv.at[i, pl.ds(first_row, rows), :], load_sems.at[i]
        )
        for i, src in enumerate((k_hbm, v_hbm))
    ]
    for copy in loads:
        copy.start()
    w_copy = pltpu.make_async_copy(w_hbm, w, w_sem)
    w_copy.start()

    barrier = pltpu.get_barrier_semaphore()
    for r in range(1, chips):
        peer = ((chip + r) % chips) * 2 + core
        pl.semaphore_signal(barrier, inc=1, device_id={"dp": peer}, device_id_type=MESH)
    pl.semaphore_signal(barrier, inc=1, device_id={"dp": partner}, device_id_type=MESH)

    @pl.when(mp > 0)
    def _():
        pl.semaphore_signal(barrier, inc=1, device_id={"mp": mp - 1}, device_id_type=MESH)

    @pl.when(mp < n_mp - 1)
    def _():
        pl.semaphore_signal(barrier, inc=1, device_id={"mp": mp + 1}, device_id_type=MESH)

    ends = jnp.where(mp == 0, 1, 0) + jnp.where(mp == n_mp - 1, 1, 0)
    for copy in loads:
        copy.wait()
    pl.semaphore_wait(barrier, chips + 2 - ends)

    def kv_copy(block, send_sem, recv_sem, target):
        part = kv.at[:, pl.ds(pl.multiple_of(block * rows, rows), rows), :]
        return pltpu.make_async_remote_copy(
            src_ref=part, dst_ref=part, send_sem=send_sem, recv_sem=recv_sem,
            device_id={"dp": target}, device_id_type=MESH,
        )

    sends = [
        kv_copy(dp, kv_send.at[r], kv_recv.at[r], ((chip + r) % chips) * 2 + core)
        for r in range(1, chips)
    ]
    sends.append(kv_copy(dp, pass_send.at[0], pass_recv.at[0], partner))
    for copy in sends:
        copy.start()

    own_segs = seg_ref[:, pl.ds(first_row, rows)].astype(jnp.float32)
    diagonal = lax.broadcasted_iota(jnp.int32, (rows, rows), 0) == lax.broadcasted_iota(
        jnp.int32, (rows, rows), 1
    )
    query_segs = jnp.sum(
        jnp.where(diagonal, jnp.broadcast_to(own_segs, (rows, rows)), 0.0), axis=1, keepdims=True
    )
    for start in range(0, tokens, key_span):
        key_segs = seg_ref[:, start : start + key_span].astype(jnp.float32)
        key_pos = start + lax.broadcasted_iota(jnp.int32, (rows, key_span), 1)
        query_pos = first_row + lax.broadcasted_iota(jnp.int32, (rows, key_span), 0)
        allowed = (query_segs == key_segs) & (key_pos <= query_pos)
        bias[:, start : start + key_span] = jnp.where(allowed, 0.0, -1e30)

    for r in range(1, chips):
        source = ((chip + chips - r) % chips) * 2 + core
        kv_copy(source, kv_send.at[r], kv_recv.at[r], dp).wait_recv()
        forward = kv_copy(source, pass_send.at[r], pass_recv.at[r], partner)
        forward.start()
        sends.append(forward)
    for r in range(chips):
        source = ((chip + chips - r) % chips) * 2 + 1 - core
        kv_copy(source, pass_send.at[r], pass_recv.at[r], dp).wait_recv()

    scale = math.log2(math.e) / math.sqrt(HD)

    def one_head(h, carry):
        columns = pl.ds(pl.multiple_of(h * HD, HD), HD)
        q = q_ref[:, columns]
        top = total = acc = None
        for start in range(0, tokens, key_span):
            span = slice(start, start + key_span)
            scores = lax.dot_general(
                q, kv[0, span, :], (((1,), (1,)), ((), ())), preferred_element_type=jnp.float32
            )
            scores = scores * scale + bias[:, span]
            new_top = jnp.max(scores, axis=1, keepdims=True)
            if top is not None:
                new_top = jnp.maximum(top, new_top)
            probs = jnp.exp2(scores - new_top)
            part_sum = jnp.sum(probs, axis=1, keepdims=True)
            part = jnp.dot(
                probs.astype(jnp.bfloat16), kv[1, span, :], preferred_element_type=jnp.float32
            )
            if top is None:
                total, acc = part_sum, part
            else:
                fade = jnp.exp2(top - new_top)
                total, acc = total * fade + part_sum, acc * fade + part
            top = new_top
        attended[:, columns] = (acc / total).astype(jnp.bfloat16)
        return carry

    lax.fori_loop(0, heads, one_head, 0)
    w_copy.wait()

    def project(d, k):
        columns = pl.ds(pl.multiple_of(d * out_cols + k * chunk, chunk), chunk)
        return jnp.dot(attended[...], w[:, columns], preferred_element_type=jnp.float32)

    def right_copy(d, k):
        at = d * pieces + k
        return pltpu.make_async_remote_copy(
            src_ref=to_right.at[at], dst_ref=from_left.at[at],
            send_sem=right_send.at[at], recv_sem=right_recv.at[at],
            device_id={"mp": mp + 1}, device_id_type=MESH,
        )

    def left_copy(d, k):
        at = d * pieces + k
        return pltpu.make_async_remote_copy(
            src_ref=to_left.at[at], dst_ref=from_right.at[at],
            send_sem=left_send.at[at], recv_sem=left_recv.at[at],
            device_id={"mp": mp - 1}, device_id_type=MESH,
        )

    def relay(d, k, copy_of, staged, arrived, at_end):
        at = d * pieces + k
        value = project(d, k)

        @pl.when(at_end)
        def _():
            staged[at] = value.astype(jnp.bfloat16)

        @pl.when(jnp.logical_not(at_end))
        def _():
            copy_of(d, k).wait_recv()
            staged[at] = (value + arrived[at].astype(jnp.float32)).astype(jnp.bfloat16)

        copy_of(d, k).start()

    items = (n_mp - 1) * pieces

    def step(t, carry):
        right_item = t - LAG * mp
        left_item = t - LAG * (n_mp - 1 - mp)
        right_at = jnp.maximum(right_item, 0)
        left_at = jnp.maximum(left_item, 0)
        right_to = n_mp - 1 - right_at // pieces
        left_to = left_at // pieces

        @pl.when((right_item >= 0) & (right_item < items) & (right_to > mp))
        def _():
            relay(right_to, right_at % pieces, right_copy, to_right, from_left, mp == 0)

        @pl.when((left_item >= 0) & (left_item < items) & (left_to < mp))
        def _():
            relay(left_to, left_at % pieces, left_copy, to_left, from_right, mp == n_mp - 1)

        return carry

    lax.fori_loop(0, items + LAG * (n_mp - 1), step, 0)

    def finish(k, carry):
        at = mp * pieces + k
        columns = pl.ds(pl.multiple_of(k * chunk, chunk), chunk)
        value = project(mp, k)

        @pl.when(mp == 0)
        def _():
            left_copy(mp, k).wait_recv()
            out_ref[:, columns] = (value + from_right[at].astype(jnp.float32)).astype(jnp.bfloat16)

        @pl.when(mp == n_mp - 1)
        def _():
            right_copy(mp, k).wait_recv()
            out_ref[:, columns] = (value + from_left[at].astype(jnp.float32)).astype(jnp.bfloat16)

        @pl.when((mp > 0) & (mp < n_mp - 1))
        def _():
            left_copy(mp, k).wait_recv()
            right_copy(mp, k).wait_recv()
            both = from_left[at].astype(jnp.float32) + from_right[at].astype(jnp.float32)
            out_ref[:, columns] = (value + both).astype(jnp.bfloat16)

        return carry

    lax.fori_loop(0, pieces, finish, 0)

    for copy in sends:
        copy.wait_send()

    def drain(i, carry):
        s, k = i // pieces, i % pieces

        @pl.when(n_mp - 1 - s > mp)
        def _():
            right_copy(n_mp - 1 - s, k).wait_send()

        @pl.when(s < mp)
        def _():
            left_copy(s, k).wait_send()

        return carry

    lax.fori_loop(0, (n_mp - 1) * pieces, drain, 0)


def relay_call(n_dp, n_mp, segment_ids, queries, keys, values, out_weight):
    rows, tokens = queries.shape[0], segment_ids.shape[0]
    depth, width = out_weight.shape
    out_cols = width // n_mp
    chunk = min(256, out_cols)
    slots = n_mp * (out_cols // chunk)
    key_span = min(2048, tokens)
    dma = pltpu.SemaphoreType.DMA
    vmem = pl.BlockSpec(memory_space=pltpu.VMEM)
    hbm = pl.BlockSpec(memory_space=pl.ANY)
    stage = pltpu.VMEM((slots, rows, chunk), jnp.bfloat16)
    return pl.pallas_call(
        functools.partial(relay_kernel, n_dp, n_mp, key_span, chunk),
        out_shape=jax.ShapeDtypeStruct((rows, out_cols), jnp.bfloat16),
        in_specs=[vmem, vmem, hbm, hbm, hbm],
        out_specs=vmem,
        scratch_shapes=[
            pltpu.VMEM((2, tokens, HD), jnp.bfloat16),
            pltpu.VMEM((depth, width), jnp.bfloat16),
            pltpu.VMEM((rows, tokens), jnp.float32),
            pltpu.VMEM((rows, queries.shape[1]), jnp.bfloat16),
            stage, stage, stage, stage,
            dma((2,)), dma,
            dma((n_dp // 2,)), dma((n_dp // 2,)), dma((n_dp // 2,)), dma((n_dp // 2,)),
            dma((slots,)), dma((slots,)), dma((slots,)), dma((slots,)),
        ],
        compiler_params=pltpu.CompilerParams(
            collective_id=0, has_side_effects=True, vmem_limit_bytes=60 * 1024 * 1024
        ),
    )(segment_ids.reshape(1, tokens), queries, keys, values, out_weight)


def solution(mesh):
    n_dp, n_mp = mesh.shape["dp"], mesh.shape["mp"]
    call = pair_call if (n_dp, n_mp) == (8, 4) else relay_call
    on_device = functools.partial(call, n_dp, n_mp)

    return jax.shard_map(
        on_device,
        mesh=mesh,
        in_specs=(P(), P("dp", "mp"), P("dp", None), P("dp", None), P("mp", None)),
        out_specs=P("dp", "mp"),
        check_vma=False,
    )
```

```python
import functools
import math

import jax
import jax.numpy as jnp
from jax import lax
from jax.experimental import pallas as pl
from jax.experimental.pallas import tpu as pltpu
from jax.sharding import PartitionSpec as P

HD = 128
GROUP = 8
LAG = 2
OWN, FROM_X, FROM_Y, FROM_XY = range(4)
MESH = pl.DeviceIdType.MESH


def pair_kernel(
    n_dp, n_mp, piece,
    seg_hbm, q_hbm, k_hbm, v_hbm, w_hbm, out_ref,
    seg_ref, q_ref, kv, w, w_end, bias, tops, totals, sums, att,
    far_out, far_in, end_out, end_in, done,
    load_sems, w_sems, kv_send, kv_recv, pass_send, pass_recv,
    wz_send, wz_recv, wy_send, wy_recv, az_send, az_recv,
    own_send, own_recv, ax_send, ax_recv, rel_send, rel_recv,
    far_send, far_recv, end_send, end_recv, fin_send, fin_recv, keep_sem,
):
    rows = q_ref.shape[0]
    heads = q_ref.shape[1] // HD
    tokens = n_dp * rows
    out_cols = out_ref.shape[1]
    span = 4 * rows
    depth, quarter = w.shape[1], w.shape[2]
    r_count = rows // piece
    half_items = 2 * r_count
    w_chunks = 4
    chunk = depth // 2 // w_chunks
    dp, mp = lax.axis_index("dp"), lax.axis_index("mp")
    core, chip = dp % 2, dp // 2
    x, y = chip % 2, chip // 2
    partner = dp + 1 - 2 * core
    x_same, x_other = (y * 2 + 1 - x) * 2 + core, (y * 2 + 1 - x) * 2 + 1 - core
    y_same = ((1 - y) * 2 + x) * 2 + core
    first_row = pl.multiple_of(dp * rows, rows)
    left_half = mp < n_mp // 2
    is_end = (mp == 0) | (mp == n_mp - 1)
    is_mid = jnp.logical_not(is_end)
    end_mp = jnp.where(left_half, 0, n_mp - 1)
    mid_mp = jnp.where(left_half, 1, n_mp - 2)
    far_mp = n_mp - 1 - mp
    slot, slot_partner = x * 2 + core, x * 2 + 1 - core
    slot_x, slot_xo = (1 - x) * 2 + core, (1 - x) * 2 + 1 - core

    def remote(src, dst, send, recv, dp_to=None, mp_to=None):
        target = {}
        if dp_to is not None:
            target["dp"] = dp_to
        if mp_to is not None:
            target["mp"] = mp_to
        return pltpu.make_async_remote_copy(
            src_ref=src, dst_ref=dst, send_sem=send, recv_sem=recv,
            device_id=target, device_id_type=MESH,
        )

    barrier = pltpu.get_barrier_semaphore()
    for peer in (partner, x_same, x_other, y_same):
        pl.semaphore_signal(barrier, inc=1, device_id={"dp": peer}, device_id_type=MESH)

    @pl.when(mp > 0)
    def _():
        pl.semaphore_signal(barrier, inc=1, device_id={"mp": mp - 1}, device_id_type=MESH)

    @pl.when(mp < n_mp - 1)
    def _():
        pl.semaphore_signal(barrier, inc=1, device_id={"mp": mp + 1}, device_id_type=MESH)

    kv_col = pl.multiple_of((mp * heads // GROUP) * HD, HD)
    for i, src in enumerate((k_hbm, v_hbm)):
        pltpu.make_async_copy(
            src.at[:, pl.ds(kv_col, HD)], kv.at[i, pl.ds(first_row, rows), :], load_sems.at[0]
        ).start()
    own_kv = kv.at[:, pl.ds(first_row, rows), :]

    def w_load(d):
        block = jnp.where(left_half, d, n_mp - 1 - d)
        columns = pl.ds(pl.multiple_of(block * out_cols + slot * quarter, quarter), quarter)
        return pltpu.make_async_copy(
            w_hbm.at[:, columns], w.at[d], w_sems.at[0 if d == n_mp - 1 else 1]
        )

    w_load(n_mp - 1).start()
    seg_load = pltpu.make_async_copy(seg_hbm, seg_ref, load_sems.at[1])
    q_load = pltpu.make_async_copy(q_hbm, q_ref, load_sems.at[2])
    seg_load.start()
    q_load.start()
    for d in range(n_mp - 1):
        w_load(d).start()

    pltpu.make_async_copy(own_kv, own_kv, load_sems.at[0]).wait()
    pl.semaphore_wait(barrier, 6 - jnp.where(is_end, 1, 0))


    xy_same = ((1 - y) * 2 + 1 - x) * 2 + core

    def block_of(block, count=1):
        return kv.at[:, pl.ds(pl.multiple_of(block * rows, rows), count * rows), :]

    def kv_link(block, k, target):
        part = block_of(block)
        return remote(part, part, kv_send, kv_recv.at[k], target)

    def kv_pass(block, k):
        part = block_of(block)
        return remote(part, part, pass_send, pass_recv.at[k // 2], partner)

    def passed(k):
        both = block_of(0, 2)
        remote(both, both, pass_send, pass_recv.at[k // 2], partner).wait_recv()

    kv_link(dp, FROM_X, x_same).start()

    @pl.when(y == 0)
    def _():
        kv_link(dp, FROM_Y, y_same).start()

    kv_pass(dp, OWN).start()

    def w_z(j):
        d = n_mp - 1 - j // w_chunks
        at = pl.ds(pl.multiple_of(y * (depth // 2) + j % w_chunks * chunk, chunk), chunk)
        return remote(w.at[d, at, :], w_end.at[d, at, :], wz_send, wz_recv.at[j], mp_to=mid_mp)

    def w_y(j):
        d = n_mp - 1 - j // w_chunks
        at = pl.ds(pl.multiple_of(y * (depth // 2) + j % w_chunks * chunk, chunk), chunk)
        part = w_end.at[d, at, :]
        return remote(part, part, wy_send, wy_recv.at[j // w_chunks], y_same)

    def pass_w(j):
        w_z(j).wait_recv()
        w_y(j).start()

    def w_there(block):
        half = w_end.at[n_mp - 1 - block, pl.ds(0, depth // 2), :]
        remote(half, half, wy_send, wy_recv.at[block], y_same).wait_recv()

    @pl.when(is_end)
    def _():
        w_load(n_mp - 1).wait()
        for j in range(w_chunks):
            w_z(j).start()

    seg_load.wait()
    own_segs = seg_ref[:, pl.ds(first_row, rows)].astype(jnp.float32)
    diagonal = lax.broadcasted_iota(jnp.int32, (rows, rows), 0) == lax.broadcasted_iota(
        jnp.int32, (rows, rows), 1
    )
    query_segs = jnp.sum(
        jnp.where(diagonal, jnp.broadcast_to(own_segs, (rows, rows)), 0.0), axis=1, keepdims=True
    )

    def set_bias(start):
        key_segs = seg_ref[:, start : start + span].astype(jnp.float32)
        key_pos = start + lax.broadcasted_iota(jnp.int32, (rows, span), 1)
        query_pos = first_row + lax.broadcasted_iota(jnp.int32, (rows, span), 0)
        allowed = (query_segs == key_segs) & (key_pos <= query_pos)
        bias[:, start : start + span] = jnp.where(allowed, 0.0, -1e30)

    set_bias(0)

    @pl.when(y == 1)
    def _():
        set_bias(span)

    def rows_at(r):
        return pl.ds(pl.multiple_of(r * piece, piece), piece)

    def a_z(r):
        return remote(
            att.at[0, slot, rows_at(r), :], att.at[1, slot, rows_at(r), :],
            az_send, az_recv.at[r], mp_to=mid_mp,
        )

    def a_own(s, r, at):
        part = att.at[s, at, rows_at(r), :]
        return remote(part, part, own_send, own_recv.at[r], partner)

    def a_x(s, r, at):
        part = att.at[s, at, rows_at(r), :]
        return remote(part, part, ax_send, ax_recv.at[s * r_count + r], x_same)

    def a_rel(s, r, at):
        part = att.at[s, at, rows_at(r), :]
        return remote(part, part, rel_send, rel_recv.at[r], partner)

    def both_own(r):
        part = att.at[:, slot_partner, rows_at(r), :]
        remote(part, part, own_send, own_recv.at[r], partner).wait_recv()

    def both_rel(r):
        part = att.at[:, slot_xo, rows_at(r), :]
        remote(part, part, rel_send, rel_recv.at[r], partner).wait_recv()

    def pass_a(s, r):
        a_x(s, r, slot_x).wait_recv()
        a_rel(s, r, slot_x).start()

    def lhs(s, g, r):
        pair = jnp.where(g == 0, x, 1 - x) * 2
        return att[s, pl.ds(pair, 2), rows_at(r), :].reshape(2 * piece, depth)

    def product(s, g, r, d):
        weight = w if s == 0 else w_end
        return jnp.dot(lhs(s, g, r), weight[d], preferred_element_type=jnp.float32)

    def far(i):
        return remote(far_out.at[i], far_in.at[i], far_send, far_recv.at[i], mp_to=far_mp)

    def to_end(i):
        return remote(end_out.at[i], end_in.at[i], end_send, end_recv.at[i], mp_to=end_mp)

    def fin_copy(src, r, target):
        columns = pl.ds(pl.multiple_of(slot * quarter, quarter), quarter)
        return remote(src, out_ref.at[rows_at(r), columns], fin_send, fin_recv, target)

    def keep(r):
        columns = pl.ds(pl.multiple_of(slot * quarter, quarter), quarter)
        return pltpu.make_async_copy(
            done.at[0, r, core], out_ref.at[rows_at(r), columns], keep_sem
        )

    def finish(g, r, value):
        done[g, r] = value.astype(jnp.bfloat16).reshape(2, piece, quarter)

        @pl.when(g == 0)
        def _():
            fin_copy(done.at[0, r, 1 - core], r, partner).start()
            keep(r).start()

        @pl.when(g == 1)
        def _():
            fin_copy(done.at[1, r, core], r, x_same).start()
            fin_copy(done.at[1, r, 1 - core], r, x_other).start()

    def each(count, body):
        def run(i, carry):
            body(i)
            return carry

        lax.fori_loop(0, count, run, 0)

    scale = math.log2(math.e) / math.sqrt(HD)

    def attend(r, start):
        state = None
        q = jnp.concatenate([q_ref[rows_at(r), k * HD : (k + 1) * HD] for k in range(heads)])
        for at in range(start, start + span, span // 2):
            keys = slice(at, at + span // 2)
            scores = lax.dot_general(
                q, kv[0, keys, :], (((1,), (1,)), ((), ())), preferred_element_type=jnp.float32
            )
            scores = scores * scale + jnp.concatenate([bias[rows_at(r), keys]] * heads)
            new_top = jnp.max(scores, axis=1, keepdims=True)
            if state is not None:
                new_top = jnp.maximum(state[0], new_top)
            probs = jnp.exp2(scores - new_top)
            total = jnp.sum(probs, axis=1, keepdims=True)
            part = jnp.dot(
                probs.astype(jnp.bfloat16), kv[1, keys, :], preferred_element_type=jnp.float32
            )
            if state is not None:
                fade = jnp.exp2(state[0] - new_top)
                total, part = state[1] * fade + total, state[2] * fade + part
            state = new_top, total, part
        return state

    def attended(r, total, part):
        out = (part / total).astype(jnp.bfloat16)
        for k in range(heads):
            att[0, slot, rows_at(r), k * HD : (k + 1) * HD] = out[k * piece : (k + 1) * piece]

    def share(r):
        a_own(0, r, slot).start()

        @pl.when(is_end)
        def _():
            a_z(r).start()
            a_x(0, r, slot).start()

        @pl.when(is_mid & (r < 2))
        def _():
            a_x(0, r, slot).start()

        @pl.when(is_mid & (r == 3))
        def _():
            a_x(0, 2, slot).start()

    def mid_pass_w(j):
        @pl.when(is_mid)
        def _():
            pass_w(j)

    q_load.wait()

    @pl.when(y == 0)
    def _():
        kv_link(x_same, FROM_X, dp).wait_recv()
        kv_pass(x_same, FROM_X).start()
        mid_pass_w(0)
        passed(FROM_X)

        def run(r):
            top, total, part = attend(r, 0)
            attended(r, total, part)
            share(r)

            @pl.when(is_mid & (r > 0))
            def _():
                pass_w(r)

        each(r_count, run)

    @pl.when(y == 1)
    def _():
        kv_link(y_same, FROM_Y, dp).wait_recv()
        kv_link(y_same, FROM_XY, x_same).start()
        kv_pass(y_same, FROM_Y).start()
        kv_link(x_same, FROM_X, dp).wait_recv()
        kv_pass(x_same, FROM_X).start()
        mid_pass_w(0)
        passed(FROM_X)

        def begin(r):
            top, total, part = attend(r, span)
            tops[r] = jnp.broadcast_to(top, part.shape)
            totals[r] = jnp.broadcast_to(total, part.shape)
            sums[r] = part

            @pl.when(r == r_count - 2)
            def _():
                kv_link(xy_same, FROM_XY, dp).wait_recv()
                kv_pass(xy_same, FROM_XY).start()
                mid_pass_w(1)

        each(r_count, begin)
        passed(FROM_XY)

        def run(r):
            top, total, part = attend(r, 0)
            new_top = jnp.maximum(tops[r], top)
            old_fade, fade = jnp.exp2(tops[r] - new_top), jnp.exp2(top - new_top)
            attended(r, totals[r] * old_fade + total * fade, sums[r] * old_fade + part * fade)
            share(r)

            @pl.when(is_mid & (r < 2))
            def _():
                pass_w(2 + r)

        each(r_count, run)

    @pl.when(is_mid)
    def _():
        w_load(n_mp - 1).wait()

    rest = w.at[pl.ds(0, n_mp - 1)]
    pltpu.make_async_copy(rest, rest, w_sems.at[1]).wait()

    def sent(ref, sem):
        remote(ref, ref, sem, sem, partner).wait_send()

    def drain_early(slabs):
        sent(block_of(0, 2), kv_send)

        @pl.when(y == 0)
        def _():
            sent(block_of(0, 2), pass_send)

        @pl.when(y == 1)
        def _():
            sent(block_of(0, 4), pass_send)

        for sem in (own_send, ax_send, rel_send):
            sent(att.at[pl.ds(0, slabs), slot], sem)

    @pl.when(is_end)
    def _():
        each(2 * w_chunks, lambda j: w_z(w_chunks + j).start())
        each(r_count, lambda r: pass_a(0, r))
        drain_early(1)

        def ready(r):
            a_own(0, r, slot_partner).wait_recv()
            a_rel(0, r, slot_xo).wait_recv()

        each(r_count, ready)

        def last(i):
            g, r = i // r_count, i % r_count
            value = product(0, g, r, 0)
            to_end(i).wait_recv()
            finish(g, r, value + end_in[i].astype(jnp.float32))

        each(half_items, last)
        sent(att.at[0, slot], az_send)
        sent(w.at[pl.ds(0, n_mp - 1), pl.ds(0, depth // 2), :], wz_send)

    @pl.when(is_mid)
    def _():
        def last(f):
            g, r = 1 - f // r_count, f % r_count
            value = product(0, g, r, 1) + product(1, g, r, 1)
            far(half_items + f).wait_recv()
            finish(g, r, value + far_in[half_items + f].astype(jnp.float32))

        def step(i):
            second = i // half_items
            j = i % half_items
            g = jnp.where(second == 0, j // r_count, 1 - j // r_count)
            r = i % r_count

            @pl.when(i < r_count)
            def _():
                a_z(r).wait_recv()
                a_own(1, r, slot).start()
                both_own(r)

            @pl.when((i >= r_count) & (i < 2 * r_count))
            def _():
                both_rel(r)

            @pl.when(i == 0)
            def _():
                w_there(0)

            @pl.when(i == half_items)
            def _():
                w_there(1)

            d = n_mp - 1 - second
            far_out[i] = (product(0, g, r, d) + product(1, g, r, d)).astype(jnp.bfloat16)
            far(i).start()

            @pl.when(i < r_count - 1)
            def _():
                a_x(1, r, slot).start()

            @pl.when(i == r_count - 1)
            def _():
                a_x(0, r_count - 1, slot).start()

            @pl.when(i == r_count)
            def _():
                a_x(1, r_count - 1, slot).start()

            @pl.when((i >= w_chunks - 1) & (i < 2 * w_chunks - 1))
            def _():
                pass_w(i + 1)

            @pl.when((i >= 2 * w_chunks) & (i < 3 * w_chunks))
            def _():
                pass_w(i)

            @pl.when((i >= LAG) & (i < half_items + LAG))
            def _():
                k = i - LAG
                value = product(0, k // r_count, k % r_count, 0)
                far(k).wait_recv()
                end_out[k] = (value + far_in[k].astype(jnp.float32)).astype(jnp.bfloat16)
                to_end(k).start()

            @pl.when(i < r_count - 1)
            def _():
                pass_a(0, r)

            @pl.when((i >= 2) & (i < r_count + 1))
            def _():
                pass_a(1, i - 2)

            @pl.when(i == r_count + 1)
            def _():
                pass_a(0, r_count - 1)

            @pl.when(i == r_count + 2)
            def _():
                pass_a(1, r_count - 1)

            @pl.when(i >= half_items + half_items // 2)
            def _():
                @pl.when(i == half_items + half_items // 2)
                def _():
                    w_there(2)

                @pl.when(i == 2 * half_items - 1)
                def _():
                    sent(w.at[pl.ds(0, n_mp - 1), pl.ds(0, depth // 2), :], wy_send)
                    sent(end_out, end_send)
                    drain_early(2)

                f = 2 * (i - half_items - half_items // 2)
                each(2, lambda k: last(f + k))

        each(2 * half_items, step)
        sent(far_out, far_send)

    three_quarters = far_out.at[pl.ds(0, 3 * r_count // 2)]
    sent(three_quarters, fin_send)
    own_quarter = done.at[0, :, 0]
    pltpu.make_async_copy(own_quarter, own_quarter, keep_sem).wait()
    remote(three_quarters, three_quarters, fin_send, fin_recv, partner).wait_recv()


def pair_call(n_dp, n_mp, segment_ids, queries, keys, values, out_weight):
    rows, tokens = queries.shape[0], segment_ids.shape[0]
    depth, width = out_weight.shape
    out_cols = width // n_mp
    quarter = out_cols // 4
    heads = queries.shape[1] // HD
    piece = rows // 4
    count = rows // piece
    items = 2 * count
    dma = pltpu.SemaphoreType.DMA
    hbm = pl.BlockSpec(memory_space=pl.ANY)

    def buffer(*shape):
        return pltpu.VMEM(shape, jnp.bfloat16)

    return pl.pallas_call(
        functools.partial(pair_kernel, n_dp, n_mp, piece),
        out_shape=pltpu.VMEM((rows, out_cols), jnp.bfloat16),
        in_specs=[hbm] * 5,
        out_specs=hbm,
        scratch_shapes=[
            pltpu.VMEM((1, tokens), jnp.int32),
            buffer(rows, heads * HD),
            buffer(2, tokens, HD),
            buffer(n_mp, depth, quarter),
            buffer(n_mp, depth, quarter),
            pltpu.VMEM((rows, tokens), jnp.float32),
            pltpu.VMEM((count, heads * piece, HD), jnp.float32),
            pltpu.VMEM((count, heads * piece, HD), jnp.float32),
            pltpu.VMEM((count, heads * piece, HD), jnp.float32),
            buffer(2, 4, rows, depth),
            buffer(2 * items, 2 * piece, quarter), buffer(2 * items, 2 * piece, quarter),
            buffer(items, 2 * piece, quarter), buffer(items, 2 * piece, quarter),
            buffer(2, count, 2, piece, quarter),
            dma((3,)), dma((2,)), dma, dma((4,)), dma, dma((2,)),
            dma, dma((12,)), dma, dma((3,)), dma, dma((count,)),
            dma, dma((count,)), dma, dma((2 * count,)), dma, dma((count,)),
            dma, dma((2 * items,)), dma, dma((items,)), dma, dma, dma,
        ],
        compiler_params=pltpu.CompilerParams(
            collective_id=1, has_side_effects=True, vmem_limit_bytes=60 * 1024 * 1024
        ),
    )(segment_ids.reshape(1, tokens), queries, keys, values, out_weight)


def relay_kernel(
    n_dp, n_mp, key_span, chunk,
    seg_ref, q_ref, k_hbm, v_hbm, w_hbm, out_ref,
    kv, w, bias, attended, from_left, from_right, to_right, to_left,
    load_sems, w_sem, kv_send, kv_recv, pass_send, pass_recv,
    right_send, right_recv, left_send, left_recv,
):
    rows = q_ref.shape[0]
    heads = q_ref.shape[1] // HD
    tokens = n_dp * rows
    out_cols = out_ref.shape[1]
    pieces = out_cols // chunk
    chips = n_dp // 2
    dp, mp = lax.axis_index("dp"), lax.axis_index("mp")
    core, chip = dp % 2, dp // 2
    partner = dp + 1 - 2 * core
    first_row = pl.multiple_of(dp * rows, rows)

    kv_col = pl.multiple_of((mp * heads // GROUP) * HD, HD)
    own = kv.at[:, pl.ds(first_row, rows), :]
    loads = [
        pltpu.make_async_copy(
            src.at[:, pl.ds(kv_col, HD)], kv.at[i, pl.ds(first_row, rows), :], load_sems.at[i]
        )
        for i, src in enumerate((k_hbm, v_hbm))
    ]
    for copy in loads:
        copy.start()
    w_copy = pltpu.make_async_copy(w_hbm, w, w_sem)
    w_copy.start()

    barrier = pltpu.get_barrier_semaphore()
    for r in range(1, chips):
        peer = ((chip + r) % chips) * 2 + core
        pl.semaphore_signal(barrier, inc=1, device_id={"dp": peer}, device_id_type=MESH)
    pl.semaphore_signal(barrier, inc=1, device_id={"dp": partner}, device_id_type=MESH)

    @pl.when(mp > 0)
    def _():
        pl.semaphore_signal(barrier, inc=1, device_id={"mp": mp - 1}, device_id_type=MESH)

    @pl.when(mp < n_mp - 1)
    def _():
        pl.semaphore_signal(barrier, inc=1, device_id={"mp": mp + 1}, device_id_type=MESH)

    ends = jnp.where(mp == 0, 1, 0) + jnp.where(mp == n_mp - 1, 1, 0)
    for copy in loads:
        copy.wait()
    pl.semaphore_wait(barrier, chips + 2 - ends)

    def kv_copy(block, send_sem, recv_sem, target):
        part = kv.at[:, pl.ds(pl.multiple_of(block * rows, rows), rows), :]
        return pltpu.make_async_remote_copy(
            src_ref=part, dst_ref=part, send_sem=send_sem, recv_sem=recv_sem,
            device_id={"dp": target}, device_id_type=MESH,
        )

    sends = [
        kv_copy(dp, kv_send.at[r], kv_recv.at[r], ((chip + r) % chips) * 2 + core)
        for r in range(1, chips)
    ]
    sends.append(kv_copy(dp, pass_send.at[0], pass_recv.at[0], partner))
    for copy in sends:
        copy.start()

    own_segs = seg_ref[:, pl.ds(first_row, rows)].astype(jnp.float32)
    diagonal = lax.broadcasted_iota(jnp.int32, (rows, rows), 0) == lax.broadcasted_iota(
        jnp.int32, (rows, rows), 1
    )
    query_segs = jnp.sum(
        jnp.where(diagonal, jnp.broadcast_to(own_segs, (rows, rows)), 0.0), axis=1, keepdims=True
    )
    for start in range(0, tokens, key_span):
        key_segs = seg_ref[:, start : start + key_span].astype(jnp.float32)
        key_pos = start + lax.broadcasted_iota(jnp.int32, (rows, key_span), 1)
        query_pos = first_row + lax.broadcasted_iota(jnp.int32, (rows, key_span), 0)
        allowed = (query_segs == key_segs) & (key_pos <= query_pos)
        bias[:, start : start + key_span] = jnp.where(allowed, 0.0, -1e30)

    for r in range(1, chips):
        source = ((chip + chips - r) % chips) * 2 + core
        kv_copy(source, kv_send.at[r], kv_recv.at[r], dp).wait_recv()
        forward = kv_copy(source, pass_send.at[r], pass_recv.at[r], partner)
        forward.start()
        sends.append(forward)
    for r in range(chips):
        source = ((chip + chips - r) % chips) * 2 + 1 - core
        kv_copy(source, pass_send.at[r], pass_recv.at[r], dp).wait_recv()

    scale = math.log2(math.e) / math.sqrt(HD)

    def one_head(h, carry):
        columns = pl.ds(pl.multiple_of(h * HD, HD), HD)
        q = q_ref[:, columns]
        top = total = acc = None
        for start in range(0, tokens, key_span):
            span = slice(start, start + key_span)
            scores = lax.dot_general(
                q, kv[0, span, :], (((1,), (1,)), ((), ())), preferred_element_type=jnp.float32
            )
            scores = scores * scale + bias[:, span]
            new_top = jnp.max(scores, axis=1, keepdims=True)
            if top is not None:
                new_top = jnp.maximum(top, new_top)
            probs = jnp.exp2(scores - new_top)
            part_sum = jnp.sum(probs, axis=1, keepdims=True)
            part = jnp.dot(
                probs.astype(jnp.bfloat16), kv[1, span, :], preferred_element_type=jnp.float32
            )
            if top is None:
                total, acc = part_sum, part
            else:
                fade = jnp.exp2(top - new_top)
                total, acc = total * fade + part_sum, acc * fade + part
            top = new_top
        attended[:, columns] = (acc / total).astype(jnp.bfloat16)
        return carry

    lax.fori_loop(0, heads, one_head, 0)
    w_copy.wait()

    def project(d, k):
        columns = pl.ds(pl.multiple_of(d * out_cols + k * chunk, chunk), chunk)
        return jnp.dot(attended[...], w[:, columns], preferred_element_type=jnp.float32)

    def right_copy(d, k):
        at = d * pieces + k
        return pltpu.make_async_remote_copy(
            src_ref=to_right.at[at], dst_ref=from_left.at[at],
            send_sem=right_send.at[at], recv_sem=right_recv.at[at],
            device_id={"mp": mp + 1}, device_id_type=MESH,
        )

    def left_copy(d, k):
        at = d * pieces + k
        return pltpu.make_async_remote_copy(
            src_ref=to_left.at[at], dst_ref=from_right.at[at],
            send_sem=left_send.at[at], recv_sem=left_recv.at[at],
            device_id={"mp": mp - 1}, device_id_type=MESH,
        )

    def relay(d, k, copy_of, staged, arrived, at_end):
        at = d * pieces + k
        value = project(d, k)

        @pl.when(at_end)
        def _():
            staged[at] = value.astype(jnp.bfloat16)

        @pl.when(jnp.logical_not(at_end))
        def _():
            copy_of(d, k).wait_recv()
            staged[at] = (value + arrived[at].astype(jnp.float32)).astype(jnp.bfloat16)

        copy_of(d, k).start()

    items = (n_mp - 1) * pieces

    def step(t, carry):
        right_item = t - LAG * mp
        left_item = t - LAG * (n_mp - 1 - mp)
        right_at = jnp.maximum(right_item, 0)
        left_at = jnp.maximum(left_item, 0)
        right_to = n_mp - 1 - right_at // pieces
        left_to = left_at // pieces

        @pl.when((right_item >= 0) & (right_item < items) & (right_to > mp))
        def _():
            relay(right_to, right_at % pieces, right_copy, to_right, from_left, mp == 0)

        @pl.when((left_item >= 0) & (left_item < items) & (left_to < mp))
        def _():
            relay(left_to, left_at % pieces, left_copy, to_left, from_right, mp == n_mp - 1)

        return carry

    lax.fori_loop(0, items + LAG * (n_mp - 1), step, 0)

    def finish(k, carry):
        at = mp * pieces + k
        columns = pl.ds(pl.multiple_of(k * chunk, chunk), chunk)
        value = project(mp, k)

        @pl.when(mp == 0)
        def _():
            left_copy(mp, k).wait_recv()
            out_ref[:, columns] = (value + from_right[at].astype(jnp.float32)).astype(jnp.bfloat16)

        @pl.when(mp == n_mp - 1)
        def _():
            right_copy(mp, k).wait_recv()
            out_ref[:, columns] = (value + from_left[at].astype(jnp.float32)).astype(jnp.bfloat16)

        @pl.when((mp > 0) & (mp < n_mp - 1))
        def _():
            left_copy(mp, k).wait_recv()
            right_copy(mp, k).wait_recv()
            both = from_left[at].astype(jnp.float32) + from_right[at].astype(jnp.float32)
            out_ref[:, columns] = (value + both).astype(jnp.bfloat16)

        return carry

    lax.fori_loop(0, pieces, finish, 0)

    for copy in sends:
        copy.wait_send()

    def drain(i, carry):
        s, k = i // pieces, i % pieces

        @pl.when(n_mp - 1 - s > mp)
        def _():
            right_copy(n_mp - 1 - s, k).wait_send()

        @pl.when(s < mp)
        def _():
            left_copy(s, k).wait_send()

        return carry

    lax.fori_loop(0, (n_mp - 1) * pieces, drain, 0)


def relay_call(n_dp, n_mp, segment_ids, queries, keys, values, out_weight):
    rows, tokens = queries.shape[0], segment_ids.shape[0]
    depth, width = out_weight.shape
    out_cols = width // n_mp
    chunk = min(256, out_cols)
    slots = n_mp * (out_cols // chunk)
    key_span = min(2048, tokens)
    dma = pltpu.SemaphoreType.DMA
    vmem = pl.BlockSpec(memory_space=pltpu.VMEM)
    hbm = pl.BlockSpec(memory_space=pl.ANY)
    stage = pltpu.VMEM((slots, rows, chunk), jnp.bfloat16)
    return pl.pallas_call(
        functools.partial(relay_kernel, n_dp, n_mp, key_span, chunk),
        out_shape=jax.ShapeDtypeStruct((rows, out_cols), jnp.bfloat16),
        in_specs=[vmem, vmem, hbm, hbm, hbm],
        out_specs=vmem,
        scratch_shapes=[
            pltpu.VMEM((2, tokens, HD), jnp.bfloat16),
            pltpu.VMEM((depth, width), jnp.bfloat16),
            pltpu.VMEM((rows, tokens), jnp.float32),
            pltpu.VMEM((rows, queries.shape[1]), jnp.bfloat16),
            stage, stage, stage, stage,
            dma((2,)), dma,
            dma((n_dp // 2,)), dma((n_dp // 2,)), dma((n_dp // 2,)), dma((n_dp // 2,)),
            dma((slots,)), dma((slots,)), dma((slots,)), dma((slots,)),
        ],
        compiler_params=pltpu.CompilerParams(
            collective_id=0, has_side_effects=True, vmem_limit_bytes=60 * 1024 * 1024
        ),
    )(segment_ids.reshape(1, tokens), queries, keys, values, out_weight)


def solution(mesh):
    n_dp, n_mp = mesh.shape["dp"], mesh.shape["mp"]
    call = pair_call if (n_dp, n_mp) == (8, 4) else relay_call
    on_device = functools.partial(call, n_dp, n_mp)

    return jax.shard_map(
        on_device,
        mesh=mesh,
        in_specs=(P(), P("dp", "mp"), P("dp", None), P("dp", None), P("mp", None)),
        out_specs=P("dp", "mp"),
        check_vma=False,
    )
```

```python
import functools
import math

import jax
import jax.numpy as jnp
from jax import lax
from jax.experimental import pallas as pl
from jax.experimental.pallas import tpu as pltpu
from jax.sharding import PartitionSpec as P

HD = 128
GROUP = 8
LAG = 2
OWN, FROM_X, FROM_Y, FROM_XY = range(4)
MESH = pl.DeviceIdType.MESH


def pair_kernel(
    n_dp, n_mp, piece,
    seg_hbm, q_hbm, k_hbm, v_hbm, w_hbm, out_ref,
    seg_ref, q_ref, kv, w, w_end, bias, tops, totals, sums, own_sum, att,
    far_out, far_in, end_out, end_in, done,
    load_sems, w_sems, kv_send, kv_recv, pass_send, pass_recv,
    wz_send, wz_recv, wy_send, wy_recv, az_send, az_recv,
    own_send, own_recv, ax_send, ax_recv, rel_send, rel_recv,
    far_send, far_recv, end_send, end_recv, fin_send, fin_recv, keep_sem,
):
    rows = q_ref.shape[0]
    heads = q_ref.shape[1] // HD
    tokens = n_dp * rows
    out_cols = out_ref.shape[1]
    span = 4 * rows
    depth, quarter = w.shape[1], w.shape[2]
    r_count = rows // piece
    half_items = 2 * r_count
    w_chunks = 8
    chunk = depth // 2 // w_chunks
    dp, mp = lax.axis_index("dp"), lax.axis_index("mp")
    core, chip = dp % 2, dp // 2
    x, y = chip % 2, chip // 2
    partner = dp + 1 - 2 * core
    x_same, x_other = (y * 2 + 1 - x) * 2 + core, (y * 2 + 1 - x) * 2 + 1 - core
    y_same = ((1 - y) * 2 + x) * 2 + core
    first_row = pl.multiple_of(dp * rows, rows)
    left_half = mp < n_mp // 2
    is_end = (mp == 0) | (mp == n_mp - 1)
    is_mid = jnp.logical_not(is_end)
    end_mp = jnp.where(left_half, 0, n_mp - 1)
    mid_mp = jnp.where(left_half, 1, n_mp - 2)
    far_mp = n_mp - 1 - mp
    slot, slot_partner = x * 2 + core, x * 2 + 1 - core
    slot_x, slot_xo = (1 - x) * 2 + core, (1 - x) * 2 + 1 - core

    def remote(src, dst, send, recv, dp_to=None, mp_to=None):
        target = {}
        if dp_to is not None:
            target["dp"] = dp_to
        if mp_to is not None:
            target["mp"] = mp_to
        return pltpu.make_async_remote_copy(
            src_ref=src, dst_ref=dst, send_sem=send, recv_sem=recv,
            device_id=target, device_id_type=MESH,
        )

    barrier = pltpu.get_barrier_semaphore()
    for peer in (partner, x_same, x_other, y_same):
        pl.semaphore_signal(barrier, inc=1, device_id={"dp": peer}, device_id_type=MESH)

    @pl.when(mp > 0)
    def _():
        pl.semaphore_signal(barrier, inc=1, device_id={"mp": mp - 1}, device_id_type=MESH)

    @pl.when(mp < n_mp - 1)
    def _():
        pl.semaphore_signal(barrier, inc=1, device_id={"mp": mp + 1}, device_id_type=MESH)

    kv_col = pl.multiple_of((mp * heads // GROUP) * HD, HD)
    for i, src in enumerate((k_hbm, v_hbm)):
        pltpu.make_async_copy(
            src.at[:, pl.ds(kv_col, HD)], kv.at[i, pl.ds(first_row, rows), :], load_sems.at[0]
        ).start()
    own_kv = kv.at[:, pl.ds(first_row, rows), :]

    def w_load(d):
        block = jnp.where(left_half, d, n_mp - 1 - d)
        columns = pl.ds(pl.multiple_of(block * out_cols + slot * quarter, quarter), quarter)
        return pltpu.make_async_copy(
            w_hbm.at[:, columns], w.at[d], w_sems.at[0 if d == n_mp - 1 else 1]
        )

    w_load(n_mp - 1).start()
    seg_load = pltpu.make_async_copy(seg_hbm, seg_ref, load_sems.at[1])
    q_load = pltpu.make_async_copy(q_hbm, q_ref, load_sems.at[2])
    seg_load.start()
    q_load.start()
    for d in range(n_mp - 1):
        w_load(d).start()

    pltpu.make_async_copy(own_kv, own_kv, load_sems.at[0]).wait()
    pl.semaphore_wait(barrier, 6 - jnp.where(is_end, 1, 0))


    xy_same = ((1 - y) * 2 + 1 - x) * 2 + core

    def block_of(block, count=1):
        return kv.at[:, pl.ds(pl.multiple_of(block * rows, rows), count * rows), :]

    def kv_link(block, k, target):
        part = block_of(block)
        return remote(part, part, kv_send, kv_recv.at[k], target)

    def kv_pass(block, k):
        part = block_of(block)
        return remote(part, part, pass_send, pass_recv.at[k // 2], partner)

    def passed(k):
        both = block_of(0, 2)
        remote(both, both, pass_send, pass_recv.at[k // 2], partner).wait_recv()

    kv_link(dp, FROM_X, x_same).start()

    @pl.when(y == 0)
    def _():
        kv_link(dp, FROM_Y, y_same).start()

    kv_pass(dp, OWN).start()

    def w_z(j):
        d = n_mp - 1 - j // w_chunks
        at = pl.ds(pl.multiple_of(y * (depth // 2) + j % w_chunks * chunk, chunk), chunk)
        return remote(w.at[d, at, :], w_end.at[d, at, :], wz_send, wz_recv.at[j], mp_to=mid_mp)

    def w_y(j):
        d = n_mp - 1 - j // w_chunks
        at = pl.ds(pl.multiple_of(y * (depth // 2) + j % w_chunks * chunk, chunk), chunk)
        part = w_end.at[d, at, :]
        return remote(part, part, wy_send, wy_recv.at[j // w_chunks], y_same)

    def pass_w(j):
        w_z(j).wait_recv()
        w_y(j).start()

    def w_there(block):
        half = w_end.at[n_mp - 1 - block, pl.ds(0, depth // 2), :]
        remote(half, half, wy_send, wy_recv.at[block], y_same).wait_recv()

    @pl.when(is_end)
    def _():
        w_load(n_mp - 1).wait()
        for j in range(w_chunks):
            w_z(j).start()

    seg_load.wait()
    own_segs = seg_ref[:, pl.ds(first_row, rows)].astype(jnp.float32)
    diagonal = lax.broadcasted_iota(jnp.int32, (rows, rows), 0) == lax.broadcasted_iota(
        jnp.int32, (rows, rows), 1
    )
    query_segs = jnp.sum(
        jnp.where(diagonal, jnp.broadcast_to(own_segs, (rows, rows)), 0.0), axis=1, keepdims=True
    )

    def set_bias(start):
        key_segs = seg_ref[:, start : start + span].astype(jnp.float32)
        key_pos = start + lax.broadcasted_iota(jnp.int32, (rows, span), 1)
        query_pos = first_row + lax.broadcasted_iota(jnp.int32, (rows, span), 0)
        allowed = (query_segs == key_segs) & (key_pos <= query_pos)
        bias[:, start : start + span] = jnp.where(allowed, 0.0, -1e30)

    set_bias(0)

    @pl.when(y == 1)
    def _():
        set_bias(span)

    def rows_at(r):
        return pl.ds(pl.multiple_of(r * piece, piece), piece)

    def a_z(r):
        return remote(
            att.at[0, slot, rows_at(r), :], att.at[1, slot, rows_at(r), :],
            az_send, az_recv.at[r], mp_to=mid_mp,
        )

    def a_own(s, r, at):
        part = att.at[s, at, rows_at(r), :]
        return remote(part, part, own_send, own_recv.at[r], partner)

    def a_x(s, r, at):
        part = att.at[s, at, rows_at(r), :]
        return remote(part, part, ax_send, ax_recv.at[s * r_count + r], x_same)

    def a_rel(s, r, at):
        part = att.at[s, at, rows_at(r), :]
        return remote(part, part, rel_send, rel_recv.at[r], partner)

    def both_own(r):
        part = att.at[:, slot_partner, rows_at(r), :]
        remote(part, part, own_send, own_recv.at[r], partner).wait_recv()

    def both_rel(r):
        part = att.at[:, slot_xo, rows_at(r), :]
        remote(part, part, rel_send, rel_recv.at[r], partner).wait_recv()

    def pass_a(s, r):
        a_x(s, r, slot_x).wait_recv()
        a_rel(s, r, slot_x).start()

    def lhs(s, g, r):
        pair = jnp.where(g == 0, x, 1 - x) * 2
        return att[s, pl.ds(pair, 2), rows_at(r), :].reshape(2 * piece, depth)

    def product(s, g, r, d):
        weight = w if s == 0 else w_end
        return jnp.dot(lhs(s, g, r), weight[d], preferred_element_type=jnp.float32)

    def far(i):
        return remote(far_out.at[i], far_in.at[i], far_send, far_recv.at[i], mp_to=far_mp)

    def far_half(i, side, sem):
        at = pl.ds(pl.multiple_of(side * piece, piece), piece)
        return remote(
            far_out.at[i, at, :], far_in.at[i, at, :], far_send, far_recv.at[sem], mp_to=far_mp
        )

    def to_end(i):
        return remote(end_out.at[i], end_in.at[i], end_send, end_recv.at[i], mp_to=end_mp)

    def fin_copy(src, r, target):
        columns = pl.ds(pl.multiple_of(slot * quarter, quarter), quarter)
        return remote(src, out_ref.at[rows_at(r), columns], fin_send, fin_recv, target)

    def keep(r):
        columns = pl.ds(pl.multiple_of(slot * quarter, quarter), quarter)
        return pltpu.make_async_copy(
            done.at[0, r, core], out_ref.at[rows_at(r), columns], keep_sem
        )

    def finish(g, r, value):
        done[g, r] = value.astype(jnp.bfloat16).reshape(2, piece, quarter)

        @pl.when(g == 0)
        def _():
            fin_copy(done.at[0, r, 1 - core], r, partner).start()
            keep(r).start()

        @pl.when(g == 1)
        def _():
            fin_copy(done.at[1, r, core], r, x_same).start()
            fin_copy(done.at[1, r, 1 - core], r, x_other).start()

    def each(count, body):
        def run(i, carry):
            body(i)
            return carry

        lax.fori_loop(0, count, run, 0)

    scale = math.log2(math.e) / math.sqrt(HD)

    def attend(r, start):
        state = None
        q = jnp.concatenate([q_ref[rows_at(r), k * HD : (k + 1) * HD] for k in range(heads)])
        for at in range(start, start + span, span // 2):
            keys = slice(at, at + span // 2)
            scores = lax.dot_general(
                q, kv[0, keys, :], (((1,), (1,)), ((), ())), preferred_element_type=jnp.float32
            )
            scores = scores * scale + jnp.concatenate([bias[rows_at(r), keys]] * heads)
            new_top = jnp.max(scores, axis=1, keepdims=True)
            if state is not None:
                new_top = jnp.maximum(state[0], new_top)
            probs = jnp.exp2(scores - new_top)
            total = jnp.sum(probs, axis=1, keepdims=True)
            part = jnp.dot(
                probs.astype(jnp.bfloat16), kv[1, keys, :], preferred_element_type=jnp.float32
            )
            if state is not None:
                fade = jnp.exp2(state[0] - new_top)
                total, part = state[1] * fade + total, state[2] * fade + part
            state = new_top, total, part
        return state

    def attended(r, total, part):
        out = (part / total).astype(jnp.bfloat16)
        for k in range(heads):
            att[0, slot, rows_at(r), k * HD : (k + 1) * HD] = out[k * piece : (k + 1) * piece]

    def share(r):
        a_own(0, r, slot).start()

        @pl.when(is_end)
        def _():
            a_z(r).start()
            a_x(0, r, slot).start()

        @pl.when(is_mid & (r < 2))
        def _():
            a_x(0, r, slot).start()

        @pl.when(is_mid & (r == 3))
        def _():
            a_x(0, 2, slot).start()

    def mid_pass_w(j):
        @pl.when(is_mid)
        def _():
            pass_w(j)

    q_load.wait()

    @pl.when(y == 0)
    def _():
        mid_pass_w(0)
        kv_link(x_same, FROM_X, dp).wait_recv()
        kv_pass(x_same, FROM_X).start()
        mid_pass_w(1)
        passed(FROM_X)

        def run(r):
            top, total, part = attend(r, 0)
            attended(r, total, part)
            mid_pass_w(2 + r)
            share(r)

        each(r_count, run)
        mid_pass_w(6)
        mid_pass_w(7)

    @pl.when(y == 1)
    def _():
        mid_pass_w(0)
        kv_link(y_same, FROM_Y, dp).wait_recv()
        kv_link(y_same, FROM_XY, x_same).start()
        kv_pass(y_same, FROM_Y).start()
        mid_pass_w(1)
        kv_link(x_same, FROM_X, dp).wait_recv()
        kv_pass(x_same, FROM_X).start()
        passed(FROM_X)

        def begin(r):
            top, total, part = attend(r, span)
            tops[r] = jnp.broadcast_to(top, part.shape)
            totals[r] = jnp.broadcast_to(total, part.shape)
            sums[r] = part

            @pl.when(r == r_count - 2)
            def _():
                kv_link(xy_same, FROM_XY, dp).wait_recv()
                kv_pass(xy_same, FROM_XY).start()

            mid_pass_w(2 + r)

        each(r_count, begin)
        passed(FROM_XY)

        def run(r):
            top, total, part = attend(r, 0)
            new_top = jnp.maximum(tops[r], top)
            old_fade, fade = jnp.exp2(tops[r] - new_top), jnp.exp2(top - new_top)
            attended(r, totals[r] * old_fade + total * fade, sums[r] * old_fade + part * fade)

            @pl.when(is_mid & (r < 2))
            def _():
                pass_w(6 + r)

            share(r)

        each(r_count, run)

    @pl.when(is_mid)
    def _():
        w_load(n_mp - 1).wait()

    rest = w.at[pl.ds(0, n_mp - 1)]
    pltpu.make_async_copy(rest, rest, w_sems.at[1]).wait()

    def sent(ref, sem):
        remote(ref, ref, sem, sem, partner).wait_send()

    def drain_early(slabs):
        sent(block_of(0, 2), kv_send)

        @pl.when(y == 0)
        def _():
            sent(block_of(0, 2), pass_send)

        @pl.when(y == 1)
        def _():
            sent(block_of(0, 4), pass_send)

        for sem in (own_send, ax_send, rel_send):
            sent(att.at[pl.ds(0, slabs), slot], sem)

    @pl.when(is_end)
    def _():
        each(2 * w_chunks, lambda j: w_z(w_chunks + j).start())
        each(r_count, lambda r: pass_a(0, r))
        drain_early(1)

        def ready(r):
            a_own(0, r, slot_partner).wait_recv()
            a_rel(0, r, slot_xo).wait_recv()

        each(r_count, ready)

        def last(i):
            g, r = i // r_count, i % r_count
            value = product(0, g, r, 0)
            to_end(i).wait_recv()
            finish(g, r, value + end_in[i].astype(jnp.float32))

        each(half_items, last)
        sent(att.at[0, slot], az_send)
        sent(w.at[pl.ds(0, n_mp - 1), pl.ds(0, depth // 2), :], wz_send)

    @pl.when(is_mid)
    def _():
        def last(f):
            g, r = 1 - f // r_count, f % r_count
            value = product(0, g, r, 1) + product(1, g, r, 1)

            @pl.when(f < half_items - 1)
            def _():
                far(half_items + f).wait_recv()
                finish(g, r, value + far_in[half_items + f].astype(jnp.float32))

            @pl.when(f == half_items - 1)
            def _():
                i = 2 * half_items - 1
                own_sum[...] = value
                for side, sem, copy in (
                    (1 - core, i, fin_copy(done.at[0, r, 1 - core], r, partner)),
                    (core, i + 1, keep(r)),
                ):
                    at = pl.ds(pl.multiple_of(side * piece, piece), piece)
                    far_half(i, side, sem).wait_recv()
                    done[0, r, side] = (
                        own_sum[at, :] + far_in[i, at, :].astype(jnp.float32)
                    ).astype(jnp.bfloat16)
                    copy.start()

        def half_item(i, at, side):
            rows_r = rows_at(i)
            value = jnp.dot(
                att[0, at, rows_r, :], w[n_mp - 1], preferred_element_type=jnp.float32
            ) + jnp.dot(
                att[1, at, rows_r, :], w_end[n_mp - 1], preferred_element_type=jnp.float32
            )
            far_out[i, pl.ds(pl.multiple_of(side * piece, piece), piece), :] = value.astype(
                jnp.bfloat16
            )
            far_half(i, side, i).start()

        def step(i):
            second = i // half_items
            j = i % half_items
            g = jnp.where(second == 0, j // r_count, 1 - j // r_count)
            r = i % r_count

            @pl.when(i < r_count)
            def _():
                a_z(r).wait_recv()
                a_own(1, r, slot).start()

            @pl.when((i >= r_count) & (i < 2 * r_count))
            def _():
                both_rel(r)

            @pl.when(i == 0)
            def _():
                w_there(0)

            @pl.when(i == half_items)
            def _():
                w_there(1)

            @pl.when(i < r_count)
            def _():
                half_item(i, slot, core)
                both_own(r)
                half_item(i, slot_partner, 1 - core)

            @pl.when(i >= r_count)
            def _():
                d = n_mp - 1 - second
                far_out[i] = (product(0, g, r, d) + product(1, g, r, d)).astype(jnp.bfloat16)

            @pl.when((i >= r_count) & (i < 2 * half_items - 1))
            def _():
                far(i).start()

            @pl.when(i == 2 * half_items - 1)
            def _():
                far_half(i, 1 - core, i).start()
                far_half(i, core, i + 1).start()

            @pl.when(i < r_count - 1)
            def _():
                a_x(1, r, slot).start()
                pass_a(0, r)

            @pl.when(i == r_count - 1)
            def _():
                a_x(0, r_count - 1, slot).start()

            @pl.when(i == r_count)
            def _():
                a_x(1, r_count - 1, slot).start()

            @pl.when((i >= r_count - 1) & (i < 2 * r_count - 2))
            def _():
                pass_a(1, i - (r_count - 1))

            @pl.when(i == 2 * r_count - 2)
            def _():
                pass_a(0, r_count - 1)
                pass_a(1, r_count - 1)

            @pl.when(((i >= 3) & (i < 7)) | ((i >= 8) & (i < 12)))
            def _():
                first = 2 * i + jnp.where(i < 7, 2, 0)
                pass_w(first)
                pass_w(first + 1)

            @pl.when((i >= LAG) & (i < half_items + LAG))
            def _():
                k = i - LAG
                value = product(0, k // r_count, k % r_count, 0)
                far(k).wait_recv()
                end_out[k] = (value + far_in[k].astype(jnp.float32)).astype(jnp.bfloat16)
                to_end(k).start()

            @pl.when(i >= half_items + half_items // 2)
            def _():
                @pl.when(i == half_items + half_items // 2)
                def _():
                    w_there(2)

                @pl.when(i == 2 * half_items - 1)
                def _():
                    sent(w.at[pl.ds(0, n_mp - 1), pl.ds(0, depth // 2), :], wy_send)
                    sent(end_out, end_send)
                    drain_early(2)

                f = 2 * (i - half_items - half_items // 2)
                each(2, lambda k: last(f + k))

        each(2 * half_items, step)
        sent(far_out, far_send)

    three_quarters = far_out.at[pl.ds(0, 3 * r_count // 2)]
    sent(three_quarters, fin_send)
    own_quarter = done.at[0, :, 0]
    pltpu.make_async_copy(own_quarter, own_quarter, keep_sem).wait()
    remote(three_quarters, three_quarters, fin_send, fin_recv, partner).wait_recv()


def pair_call(n_dp, n_mp, segment_ids, queries, keys, values, out_weight):
    rows, tokens = queries.shape[0], segment_ids.shape[0]
    depth, width = out_weight.shape
    out_cols = width // n_mp
    quarter = out_cols // 4
    heads = queries.shape[1] // HD
    piece = rows // 4
    count = rows // piece
    items = 2 * count
    dma = pltpu.SemaphoreType.DMA
    hbm = pl.BlockSpec(memory_space=pl.ANY)

    def buffer(*shape):
        return pltpu.VMEM(shape, jnp.bfloat16)

    return pl.pallas_call(
        functools.partial(pair_kernel, n_dp, n_mp, piece),
        out_shape=pltpu.VMEM((rows, out_cols), jnp.bfloat16),
        in_specs=[hbm] * 5,
        out_specs=hbm,
        scratch_shapes=[
            pltpu.VMEM((1, tokens), jnp.int32),
            buffer(rows, heads * HD),
            buffer(2, tokens, HD),
            buffer(n_mp, depth, quarter),
            buffer(n_mp, depth, quarter),
            pltpu.VMEM((rows, tokens), jnp.float32),
            pltpu.VMEM((count, heads * piece, HD), jnp.float32),
            pltpu.VMEM((count, heads * piece, HD), jnp.float32),
            pltpu.VMEM((count, heads * piece, HD), jnp.float32),
            pltpu.VMEM((2 * piece, quarter), jnp.float32),
            buffer(2, 4, rows, depth),
            buffer(2 * items, 2 * piece, quarter), buffer(2 * items, 2 * piece, quarter),
            buffer(items, 2 * piece, quarter), buffer(items, 2 * piece, quarter),
            buffer(2, count, 2, piece, quarter),
            dma((3,)), dma((2,)), dma, dma((4,)), dma, dma((2,)),
            dma, dma((24,)), dma, dma((3,)), dma, dma((count,)),
            dma, dma((count,)), dma, dma((2 * count,)), dma, dma((count,)),
            dma, dma((2 * items + 1,)), dma, dma((items,)), dma, dma, dma,
        ],
        compiler_params=pltpu.CompilerParams(
            collective_id=1, has_side_effects=True, vmem_limit_bytes=60 * 1024 * 1024
        ),
    )(segment_ids.reshape(1, tokens), queries, keys, values, out_weight)


def relay_kernel(
    n_dp, n_mp, key_span, chunk,
    seg_ref, q_ref, k_hbm, v_hbm, w_hbm, out_ref,
    kv, w, bias, attended, from_left, from_right, to_right, to_left,
    load_sems, w_sem, kv_send, kv_recv, pass_send, pass_recv,
    right_send, right_recv, left_send, left_recv,
):
    rows = q_ref.shape[0]
    heads = q_ref.shape[1] // HD
    tokens = n_dp * rows
    out_cols = out_ref.shape[1]
    pieces = out_cols // chunk
    chips = n_dp // 2
    dp, mp = lax.axis_index("dp"), lax.axis_index("mp")
    core, chip = dp % 2, dp // 2
    partner = dp + 1 - 2 * core
    first_row = pl.multiple_of(dp * rows, rows)

    kv_col = pl.multiple_of((mp * heads // GROUP) * HD, HD)
    own = kv.at[:, pl.ds(first_row, rows), :]
    loads = [
        pltpu.make_async_copy(
            src.at[:, pl.ds(kv_col, HD)], kv.at[i, pl.ds(first_row, rows), :], load_sems.at[i]
        )
        for i, src in enumerate((k_hbm, v_hbm))
    ]
    for copy in loads:
        copy.start()
    w_copy = pltpu.make_async_copy(w_hbm, w, w_sem)
    w_copy.start()

    barrier = pltpu.get_barrier_semaphore()
    for r in range(1, chips):
        peer = ((chip + r) % chips) * 2 + core
        pl.semaphore_signal(barrier, inc=1, device_id={"dp": peer}, device_id_type=MESH)
    pl.semaphore_signal(barrier, inc=1, device_id={"dp": partner}, device_id_type=MESH)

    @pl.when(mp > 0)
    def _():
        pl.semaphore_signal(barrier, inc=1, device_id={"mp": mp - 1}, device_id_type=MESH)

    @pl.when(mp < n_mp - 1)
    def _():
        pl.semaphore_signal(barrier, inc=1, device_id={"mp": mp + 1}, device_id_type=MESH)

    ends = jnp.where(mp == 0, 1, 0) + jnp.where(mp == n_mp - 1, 1, 0)
    for copy in loads:
        copy.wait()
    pl.semaphore_wait(barrier, chips + 2 - ends)

    def kv_copy(block, send_sem, recv_sem, target):
        part = kv.at[:, pl.ds(pl.multiple_of(block * rows, rows), rows), :]
        return pltpu.make_async_remote_copy(
            src_ref=part, dst_ref=part, send_sem=send_sem, recv_sem=recv_sem,
            device_id={"dp": target}, device_id_type=MESH,
        )

    sends = [
        kv_copy(dp, kv_send.at[r], kv_recv.at[r], ((chip + r) % chips) * 2 + core)
        for r in range(1, chips)
    ]
    sends.append(kv_copy(dp, pass_send.at[0], pass_recv.at[0], partner))
    for copy in sends:
        copy.start()

    own_segs = seg_ref[:, pl.ds(first_row, rows)].astype(jnp.float32)
    diagonal = lax.broadcasted_iota(jnp.int32, (rows, rows), 0) == lax.broadcasted_iota(
        jnp.int32, (rows, rows), 1
    )
    query_segs = jnp.sum(
        jnp.where(diagonal, jnp.broadcast_to(own_segs, (rows, rows)), 0.0), axis=1, keepdims=True
    )
    for start in range(0, tokens, key_span):
        key_segs = seg_ref[:, start : start + key_span].astype(jnp.float32)
        key_pos = start + lax.broadcasted_iota(jnp.int32, (rows, key_span), 1)
        query_pos = first_row + lax.broadcasted_iota(jnp.int32, (rows, key_span), 0)
        allowed = (query_segs == key_segs) & (key_pos <= query_pos)
        bias[:, start : start + key_span] = jnp.where(allowed, 0.0, -1e30)

    for r in range(1, chips):
        source = ((chip + chips - r) % chips) * 2 + core
        kv_copy(source, kv_send.at[r], kv_recv.at[r], dp).wait_recv()
        forward = kv_copy(source, pass_send.at[r], pass_recv.at[r], partner)
        forward.start()
        sends.append(forward)
    for r in range(chips):
        source = ((chip + chips - r) % chips) * 2 + 1 - core
        kv_copy(source, pass_send.at[r], pass_recv.at[r], dp).wait_recv()

    scale = math.log2(math.e) / math.sqrt(HD)

    def one_head(h, carry):
        columns = pl.ds(pl.multiple_of(h * HD, HD), HD)
        q = q_ref[:, columns]
        top = total = acc = None
        for start in range(0, tokens, key_span):
            span = slice(start, start + key_span)
            scores = lax.dot_general(
                q, kv[0, span, :], (((1,), (1,)), ((), ())), preferred_element_type=jnp.float32
            )
            scores = scores * scale + bias[:, span]
            new_top = jnp.max(scores, axis=1, keepdims=True)
            if top is not None:
                new_top = jnp.maximum(top, new_top)
            probs = jnp.exp2(scores - new_top)
            part_sum = jnp.sum(probs, axis=1, keepdims=True)
            part = jnp.dot(
                probs.astype(jnp.bfloat16), kv[1, span, :], preferred_element_type=jnp.float32
            )
            if top is None:
                total, acc = part_sum, part
            else:
                fade = jnp.exp2(top - new_top)
                total, acc = total * fade + part_sum, acc * fade + part
            top = new_top
        attended[:, columns] = (acc / total).astype(jnp.bfloat16)
        return carry

    lax.fori_loop(0, heads, one_head, 0)
    w_copy.wait()

    def project(d, k):
        columns = pl.ds(pl.multiple_of(d * out_cols + k * chunk, chunk), chunk)
        return jnp.dot(attended[...], w[:, columns], preferred_element_type=jnp.float32)

    def right_copy(d, k):
        at = d * pieces + k
        return pltpu.make_async_remote_copy(
            src_ref=to_right.at[at], dst_ref=from_left.at[at],
            send_sem=right_send.at[at], recv_sem=right_recv.at[at],
            device_id={"mp": mp + 1}, device_id_type=MESH,
        )

    def left_copy(d, k):
        at = d * pieces + k
        return pltpu.make_async_remote_copy(
            src_ref=to_left.at[at], dst_ref=from_right.at[at],
            send_sem=left_send.at[at], recv_sem=left_recv.at[at],
            device_id={"mp": mp - 1}, device_id_type=MESH,
        )

    def relay(d, k, copy_of, staged, arrived, at_end):
        at = d * pieces + k
        value = project(d, k)

        @pl.when(at_end)
        def _():
            staged[at] = value.astype(jnp.bfloat16)

        @pl.when(jnp.logical_not(at_end))
        def _():
            copy_of(d, k).wait_recv()
            staged[at] = (value + arrived[at].astype(jnp.float32)).astype(jnp.bfloat16)

        copy_of(d, k).start()

    items = (n_mp - 1) * pieces

    def step(t, carry):
        right_item = t - LAG * mp
        left_item = t - LAG * (n_mp - 1 - mp)
        right_at = jnp.maximum(right_item, 0)
        left_at = jnp.maximum(left_item, 0)
        right_to = n_mp - 1 - right_at // pieces
        left_to = left_at // pieces

        @pl.when((right_item >= 0) & (right_item < items) & (right_to > mp))
        def _():
            relay(right_to, right_at % pieces, right_copy, to_right, from_left, mp == 0)

        @pl.when((left_item >= 0) & (left_item < items) & (left_to < mp))
        def _():
            relay(left_to, left_at % pieces, left_copy, to_left, from_right, mp == n_mp - 1)

        return carry

    lax.fori_loop(0, items + LAG * (n_mp - 1), step, 0)

    def finish(k, carry):
        at = mp * pieces + k
        columns = pl.ds(pl.multiple_of(k * chunk, chunk), chunk)
        value = project(mp, k)

        @pl.when(mp == 0)
        def _():
            left_copy(mp, k).wait_recv()
            out_ref[:, columns] = (value + from_right[at].astype(jnp.float32)).astype(jnp.bfloat16)

        @pl.when(mp == n_mp - 1)
        def _():
            right_copy(mp, k).wait_recv()
            out_ref[:, columns] = (value + from_left[at].astype(jnp.float32)).astype(jnp.bfloat16)

        @pl.when((mp > 0) & (mp < n_mp - 1))
        def _():
            left_copy(mp, k).wait_recv()
            right_copy(mp, k).wait_recv()
            both = from_left[at].astype(jnp.float32) + from_right[at].astype(jnp.float32)
            out_ref[:, columns] = (value + both).astype(jnp.bfloat16)

        return carry

    lax.fori_loop(0, pieces, finish, 0)

    for copy in sends:
        copy.wait_send()

    def drain(i, carry):
        s, k = i // pieces, i % pieces

        @pl.when(n_mp - 1 - s > mp)
        def _():
            right_copy(n_mp - 1 - s, k).wait_send()

        @pl.when(s < mp)
        def _():
            left_copy(s, k).wait_send()

        return carry

    lax.fori_loop(0, (n_mp - 1) * pieces, drain, 0)


def relay_call(n_dp, n_mp, segment_ids, queries, keys, values, out_weight):
    rows, tokens = queries.shape[0], segment_ids.shape[0]
    depth, width = out_weight.shape
    out_cols = width // n_mp
    chunk = min(256, out_cols)
    slots = n_mp * (out_cols // chunk)
    key_span = min(2048, tokens)
    dma = pltpu.SemaphoreType.DMA
    vmem = pl.BlockSpec(memory_space=pltpu.VMEM)
    hbm = pl.BlockSpec(memory_space=pl.ANY)
    stage = pltpu.VMEM((slots, rows, chunk), jnp.bfloat16)
    return pl.pallas_call(
        functools.partial(relay_kernel, n_dp, n_mp, key_span, chunk),
        out_shape=jax.ShapeDtypeStruct((rows, out_cols), jnp.bfloat16),
        in_specs=[vmem, vmem, hbm, hbm, hbm],
        out_specs=vmem,
        scratch_shapes=[
            pltpu.VMEM((2, tokens, HD), jnp.bfloat16),
            pltpu.VMEM((depth, width), jnp.bfloat16),
            pltpu.VMEM((rows, tokens), jnp.float32),
            pltpu.VMEM((rows, queries.shape[1]), jnp.bfloat16),
            stage, stage, stage, stage,
            dma((2,)), dma,
            dma((n_dp // 2,)), dma((n_dp // 2,)), dma((n_dp // 2,)), dma((n_dp // 2,)),
            dma((slots,)), dma((slots,)), dma((slots,)), dma((slots,)),
        ],
        compiler_params=pltpu.CompilerParams(
            collective_id=0, has_side_effects=True, vmem_limit_bytes=60 * 1024 * 1024
        ),
    )(segment_ids.reshape(1, tokens), queries, keys, values, out_weight)


def solution(mesh):
    n_dp, n_mp = mesh.shape["dp"], mesh.shape["mp"]
    call = pair_call if (n_dp, n_mp) == (8, 4) else relay_call
    on_device = functools.partial(call, n_dp, n_mp)

    return jax.shard_map(
        on_device,
        mesh=mesh,
        in_specs=(P(), P("dp", "mp"), P("dp", None), P("dp", None), P("mp", None)),
        out_specs=P("dp", "mp"),
        check_vma=False,
    )
```

```python
import functools
import math

import jax
import jax.numpy as jnp
from jax import lax
from jax.experimental import pallas as pl
from jax.experimental.pallas import tpu as pltpu
from jax.sharding import PartitionSpec as P

HD = 128
GROUP = 8
LAG = 3
OWN, FROM_X, FROM_Y, FROM_XY = range(4)
MESH = pl.DeviceIdType.MESH


def pair_kernel(
    n_dp, n_mp, piece,
    seg_hbm, q_hbm, k_hbm, v_hbm, w_hbm, out_ref,
    seg_ref, q_ref, kv, w, w_end, bias, tops, totals, sums, own_sum, att,
    far_out, far_in, end_out, end_in, done,
    load_sems, w_sems, kv_send, kv_recv, pass_send, pass_recv,
    wz_send, wz_recv, both_send, both_recv, wy_send, wy_recv, az_send, az_recv,
    own_send, own_recv, ax_send, ax_recv, rel_send, rel_recv,
    far_send, far_recv, end_send, end_recv, fin_send, fin_recv, keep_sem,
):
    rows = q_ref.shape[0]
    heads = q_ref.shape[1] // HD
    tokens = n_dp * rows
    out_cols = out_ref.shape[1]
    span = 4 * rows
    depth, quarter = w.shape[1], w.shape[2]
    r_count = rows // piece
    half_items = 2 * r_count
    w_chunks = 8
    chunk = depth // 2 // w_chunks
    dp, mp = lax.axis_index("dp"), lax.axis_index("mp")
    core, chip = dp % 2, dp // 2
    x, y = chip % 2, chip // 2
    partner = dp + 1 - 2 * core
    x_same, x_other = (y * 2 + 1 - x) * 2 + core, (y * 2 + 1 - x) * 2 + 1 - core
    y_same = ((1 - y) * 2 + x) * 2 + core
    first_row = pl.multiple_of(dp * rows, rows)
    left_half = mp < n_mp // 2
    is_end = (mp == 0) | (mp == n_mp - 1)
    is_mid = jnp.logical_not(is_end)
    end_mp = jnp.where(left_half, 0, n_mp - 1)
    mid_mp = jnp.where(left_half, 1, n_mp - 2)
    far_mp = n_mp - 1 - mp
    slot, slot_partner = x * 2 + core, x * 2 + 1 - core
    slot_x, slot_xo = (1 - x) * 2 + core, (1 - x) * 2 + 1 - core

    def remote(src, dst, send, recv, dp_to=None, mp_to=None):
        target = {}
        if dp_to is not None:
            target["dp"] = dp_to
        if mp_to is not None:
            target["mp"] = mp_to
        return pltpu.make_async_remote_copy(
            src_ref=src, dst_ref=dst, send_sem=send, recv_sem=recv,
            device_id=target, device_id_type=MESH,
        )

    barrier = pltpu.get_barrier_semaphore()
    for peer in (partner, x_same, x_other, y_same):
        pl.semaphore_signal(barrier, inc=1, device_id={"dp": peer}, device_id_type=MESH)

    @pl.when(mp > 0)
    def _():
        pl.semaphore_signal(barrier, inc=1, device_id={"mp": mp - 1}, device_id_type=MESH)

    @pl.when(mp < n_mp - 1)
    def _():
        pl.semaphore_signal(barrier, inc=1, device_id={"mp": mp + 1}, device_id_type=MESH)

    kv_col = pl.multiple_of((mp * heads // GROUP) * HD, HD)
    for i, src in enumerate((k_hbm, v_hbm)):
        pltpu.make_async_copy(
            src.at[:, pl.ds(kv_col, HD)], kv.at[i, pl.ds(first_row, rows), :], load_sems.at[0]
        ).start()
    own_kv = kv.at[:, pl.ds(first_row, rows), :]

    def w_load(d):
        block = jnp.where(left_half, d, n_mp - 1 - d)
        columns = pl.ds(pl.multiple_of(block * out_cols + slot * quarter, quarter), quarter)
        return pltpu.make_async_copy(
            w_hbm.at[:, columns], w.at[d], w_sems.at[0 if d == n_mp - 1 else 1]
        )

    w_load(n_mp - 1).start()
    seg_load = pltpu.make_async_copy(seg_hbm, seg_ref, load_sems.at[1])
    q_load = pltpu.make_async_copy(q_hbm, q_ref, load_sems.at[2])
    seg_load.start()
    q_load.start()
    pltpu.make_async_copy(own_kv, own_kv, load_sems.at[0]).wait()
    pl.semaphore_wait(barrier, 6 - jnp.where(is_end, 1, 0))


    xy_same = ((1 - y) * 2 + 1 - x) * 2 + core

    def block_of(block, count=1):
        return kv.at[:, pl.ds(pl.multiple_of(block * rows, rows), count * rows), :]

    def kv_link(block, k, target):
        part = block_of(block)
        return remote(part, part, kv_send, kv_recv.at[k], target)

    def kv_pass(block, k):
        part = block_of(block)
        return remote(part, part, pass_send, pass_recv.at[k // 2], partner)

    def passed(k):
        both = block_of(0, 2)
        remote(both, both, pass_send, pass_recv.at[k // 2], partner).wait_recv()

    kv_link(dp, FROM_X, x_same).start()

    @pl.when(y == 0)
    def _():
        kv_link(dp, FROM_Y, y_same).start()

    kv_pass(dp, OWN).start()

    def w_z(j):
        d = n_mp - 1 - j // w_chunks
        at = pl.ds(pl.multiple_of(y * (depth // 2) + j % w_chunks * chunk, chunk), chunk)
        return remote(w.at[d, at, :], w_end.at[d, at, :], wz_send, wz_recv.at[j], mp_to=mid_mp)

    def w_y(j):
        d = n_mp - 1 - j // w_chunks
        at = pl.ds(pl.multiple_of(y * (depth // 2) + j % w_chunks * chunk, chunk), chunk)
        part = w_end.at[d, at, :]
        return remote(part, part, wy_send, wy_recv.at[j // w_chunks], y_same)

    direct = 2 * w_chunks - w_chunks // 4
    direct_rows = w_chunks // 4 * chunk

    def w_both(side):
        start = (1 + side) * (depth // 2) - direct_rows
        at = pl.ds(pl.multiple_of(start, direct_rows), direct_rows)
        return remote(
            w.at[n_mp - 2, at, :], w_end.at[n_mp - 2, at, :], both_send, both_recv, mp_to=mid_mp
        )

    def pass_w(j):
        w_z(j).wait_recv()

        @pl.when((j < direct) | (j >= 2 * w_chunks))
        def _():
            w_y(j).start()

    def w_there(block):
        count = depth // 2 - (direct_rows if block == 1 else 0)
        part = w_end.at[n_mp - 1 - block, pl.ds(0, count), :]
        remote(part, part, wy_send, wy_recv.at[block], y_same).wait_recv()
        if block == 1:
            w_both(1 - y).wait_recv()

    @pl.when(is_end)
    def _():
        w_load(n_mp - 1).wait()
        for j in range(w_chunks):
            w_z(j).start()

    for d in range(n_mp - 1):
        w_load(d).start()

    seg_load.wait()
    own_segs = seg_ref[:, pl.ds(first_row, rows)].astype(jnp.float32)
    diagonal = lax.broadcasted_iota(jnp.int32, (rows, rows), 0) == lax.broadcasted_iota(
        jnp.int32, (rows, rows), 1
    )
    query_segs = jnp.sum(
        jnp.where(diagonal, jnp.broadcast_to(own_segs, (rows, rows)), 0.0), axis=1, keepdims=True
    )

    def set_bias(start):
        key_segs = seg_ref[:, start : start + span].astype(jnp.float32)
        key_pos = start + lax.broadcasted_iota(jnp.int32, (rows, span), 1)
        query_pos = first_row + lax.broadcasted_iota(jnp.int32, (rows, span), 0)
        allowed = (query_segs == key_segs) & (key_pos <= query_pos)
        bias[:, start : start + span] = jnp.where(allowed, 0.0, -1e30)

    set_bias(0)

    @pl.when(y == 1)
    def _():
        set_bias(span)

    def rows_at(r):
        return pl.ds(pl.multiple_of(r * piece, piece), piece)

    def a_z(r):
        return remote(
            att.at[0, slot, rows_at(r), :], att.at[1, slot, rows_at(r), :],
            az_send, az_recv.at[r], mp_to=mid_mp,
        )

    def a_own(s, r, at):
        part = att.at[s, at, rows_at(r), :]
        return remote(part, part, own_send, own_recv.at[r], partner)

    def a_x(s, r, at):
        part = att.at[s, at, rows_at(r), :]
        return remote(part, part, ax_send, ax_recv.at[s * r_count + r], x_same)

    def a_rel(s, r, at):
        part = att.at[s, at, rows_at(r), :]
        return remote(part, part, rel_send, rel_recv.at[r], partner)

    def both_own(r):
        part = att.at[:, slot_partner, rows_at(r), :]
        remote(part, part, own_send, own_recv.at[r], partner).wait_recv()

    def both_rel(r):
        part = att.at[:, slot_xo, rows_at(r), :]
        remote(part, part, rel_send, rel_recv.at[r], partner).wait_recv()

    def pass_a(s, r):
        a_x(s, r, slot_x).wait_recv()
        a_rel(s, r, slot_x).start()

    def lhs(s, g, r):
        pair = jnp.where(g == 0, x, 1 - x) * 2
        return att[s, pl.ds(pair, 2), rows_at(r), :].reshape(2 * piece, depth)

    def product(s, g, r, d):
        weight = w if s == 0 else w_end
        return jnp.dot(lhs(s, g, r), weight[d], preferred_element_type=jnp.float32)

    def far(i):
        return remote(far_out.at[i], far_in.at[i], far_send, far_recv.at[i], mp_to=far_mp)

    def far_half(i, side, sem):
        at = pl.ds(pl.multiple_of(side * piece, piece), piece)
        return remote(
            far_out.at[i, at, :], far_in.at[i, at, :], far_send, far_recv.at[sem], mp_to=far_mp
        )

    def to_end(i):
        return remote(end_out.at[i], end_in.at[i], end_send, end_recv.at[i], mp_to=end_mp)

    def fin_copy(src, r, target):
        columns = pl.ds(pl.multiple_of(slot * quarter, quarter), quarter)
        return remote(src, out_ref.at[rows_at(r), columns], fin_send, fin_recv, target)

    def keep(r):
        columns = pl.ds(pl.multiple_of(slot * quarter, quarter), quarter)
        return pltpu.make_async_copy(
            done.at[0, r, core], out_ref.at[rows_at(r), columns], keep_sem
        )

    def finish(g, r, value):
        done[g, r] = value.astype(jnp.bfloat16).reshape(2, piece, quarter)

        @pl.when(g == 0)
        def _():
            fin_copy(done.at[0, r, 1 - core], r, partner).start()
            keep(r).start()

        @pl.when(g == 1)
        def _():
            fin_copy(done.at[1, r, core], r, x_same).start()
            fin_copy(done.at[1, r, 1 - core], r, x_other).start()

    def each(count, body):
        def run(i, carry):
            body(i)
            return carry

        lax.fori_loop(0, count, run, 0)

    scale = math.log2(math.e) / math.sqrt(HD)

    def attend(r, start):
        state = None
        q = jnp.concatenate([q_ref[rows_at(r), k * HD : (k + 1) * HD] for k in range(heads)])
        for at in range(start, start + span, span // 2):
            keys = slice(at, at + span // 2)
            scores = lax.dot_general(
                q, kv[0, keys, :], (((1,), (1,)), ((), ())), preferred_element_type=jnp.float32
            )
            scores = scores * scale + jnp.concatenate([bias[rows_at(r), keys]] * heads)
            new_top = jnp.max(scores, axis=1, keepdims=True)
            if state is not None:
                new_top = jnp.maximum(state[0], new_top)
            probs = jnp.exp2(scores - new_top)
            total = jnp.sum(probs, axis=1, keepdims=True)
            part = jnp.dot(
                probs.astype(jnp.bfloat16), kv[1, keys, :], preferred_element_type=jnp.float32
            )
            if state is not None:
                fade = jnp.exp2(state[0] - new_top)
                total, part = state[1] * fade + total, state[2] * fade + part
            state = new_top, total, part
        return state

    def attended(r, total, part):
        out = (part / total).astype(jnp.bfloat16)
        for k in range(heads):
            att[0, slot, rows_at(r), k * HD : (k + 1) * HD] = out[k * piece : (k + 1) * piece]

    def share(r):
        a_own(0, r, slot).start()

        @pl.when(is_end)
        def _():
            a_z(r).start()
            a_x(0, r, slot).start()

        @pl.when(is_mid & (r < 2))
        def _():
            a_x(0, r, slot).start()

        @pl.when(is_mid & (r == 3))
        def _():
            a_x(0, 2, slot).start()

    def mid_pass_w(j):
        @pl.when(is_mid)
        def _():
            pass_w(j)

    q_load.wait()

    @pl.when(y == 0)
    def _():
        mid_pass_w(0)
        kv_link(x_same, FROM_X, dp).wait_recv()
        kv_pass(x_same, FROM_X).start()
        mid_pass_w(1)
        passed(FROM_X)

        def run(r):
            top, total, part = attend(r, 0)
            attended(r, total, part)
            mid_pass_w(2 + r)
            share(r)

        each(r_count, run)
        mid_pass_w(6)
        mid_pass_w(7)

    @pl.when(y == 1)
    def _():
        mid_pass_w(0)
        kv_link(y_same, FROM_Y, dp).wait_recv()
        kv_link(y_same, FROM_XY, x_same).start()
        kv_pass(y_same, FROM_Y).start()
        mid_pass_w(1)
        kv_link(x_same, FROM_X, dp).wait_recv()
        kv_pass(x_same, FROM_X).start()
        passed(FROM_X)

        def begin(r):
            top, total, part = attend(r, span)
            tops[r] = jnp.broadcast_to(top, part.shape)
            totals[r] = jnp.broadcast_to(total, part.shape)
            sums[r] = part

            @pl.when(r == r_count - 2)
            def _():
                kv_link(xy_same, FROM_XY, dp).wait_recv()
                kv_pass(xy_same, FROM_XY).start()

            mid_pass_w(2 + r)

        each(r_count, begin)
        passed(FROM_XY)

        def run(r):
            top, total, part = attend(r, 0)
            new_top = jnp.maximum(tops[r], top)
            old_fade, fade = jnp.exp2(tops[r] - new_top), jnp.exp2(top - new_top)
            attended(r, totals[r] * old_fade + total * fade, sums[r] * old_fade + part * fade)

            @pl.when(is_mid & (r < 2))
            def _():
                pass_w(6 + r)

            share(r)

        each(r_count, run)

    @pl.when(is_mid)
    def _():
        w_load(n_mp - 1).wait()

    rest = w.at[pl.ds(0, n_mp - 1)]
    pltpu.make_async_copy(rest, rest, w_sems.at[1]).wait()

    def sent(ref, sem):
        remote(ref, ref, sem, sem, partner).wait_send()

    def drain_early(slabs):
        sent(block_of(0, 2), kv_send)

        @pl.when(y == 0)
        def _():
            sent(block_of(0, 2), pass_send)

        @pl.when(y == 1)
        def _():
            sent(block_of(0, 4), pass_send)

        for sem in (own_send, ax_send, rel_send):
            sent(att.at[pl.ds(0, slabs), slot], sem)

    @pl.when(is_end)
    def _():
        each(w_chunks, lambda j: w_z(w_chunks + j).start())
        w_both(1 - y).start()
        each(w_chunks, lambda j: w_z(2 * w_chunks + j).start())
        each(r_count, lambda r: pass_a(0, r))
        drain_early(1)

        def ready(r):
            a_own(0, r, slot_partner).wait_recv()
            a_rel(0, r, slot_xo).wait_recv()

        each(r_count, ready)

        def last(i):
            g, r = i // r_count, i % r_count
            value = product(0, g, r, 0)
            to_end(i).wait_recv()
            finish(g, r, value + end_in[i].astype(jnp.float32))

        each(half_items, last)
        sent(att.at[0, slot], az_send)
        sent(w.at[pl.ds(0, n_mp - 1), pl.ds(0, depth // 2), :], wz_send)
        w_both(1 - y).wait_send()

    @pl.when(is_mid)
    def _():
        def last(f):
            g, r = 1 - f // r_count, f % r_count
            value = product(0, g, r, 1) + product(1, g, r, 1)

            @pl.when(f < half_items - 1)
            def _():
                far(half_items + f).wait_recv()
                finish(g, r, value + far_in[half_items + f].astype(jnp.float32))

            @pl.when(f == half_items - 1)
            def _():
                i = 2 * half_items - 1
                own_sum[...] = value
                for side, sem, copy in (
                    (1 - core, i, fin_copy(done.at[0, r, 1 - core], r, partner)),
                    (core, i + 1, keep(r)),
                ):
                    at = pl.ds(pl.multiple_of(side * piece, piece), piece)
                    far_half(i, side, sem).wait_recv()
                    done[0, r, side] = (
                        own_sum[at, :] + far_in[i, at, :].astype(jnp.float32)
                    ).astype(jnp.bfloat16)
                    copy.start()

        def half_item(i, at, side):
            rows_r = rows_at(i)
            value = jnp.dot(
                att[0, at, rows_r, :], w[n_mp - 1], preferred_element_type=jnp.float32
            ) + jnp.dot(
                att[1, at, rows_r, :], w_end[n_mp - 1], preferred_element_type=jnp.float32
            )
            far_out[i, pl.ds(pl.multiple_of(side * piece, piece), piece), :] = value.astype(
                jnp.bfloat16
            )
            far_half(i, side, i).start()

        def step(i):
            second = i // half_items
            j = i % half_items
            g = jnp.where(second == 0, j // r_count, 1 - j // r_count)
            r = i % r_count

            @pl.when(i < r_count)
            def _():
                a_z(r).wait_recv()
                a_own(1, r, slot).start()

            @pl.when((i >= r_count) & (i < 2 * r_count))
            def _():
                both_rel(r)

            @pl.when(i == 0)
            def _():
                w_there(0)

            @pl.when(i == half_items)
            def _():
                w_there(1)

            @pl.when(i < r_count)
            def _():
                half_item(i, slot, core)
                both_own(r)
                half_item(i, slot_partner, 1 - core)

            @pl.when(i >= r_count)
            def _():
                d = n_mp - 1 - second
                far_out[i] = (product(0, g, r, d) + product(1, g, r, d)).astype(jnp.bfloat16)

            @pl.when((i >= r_count) & (i < 2 * half_items - 1))
            def _():
                far(i).start()

            @pl.when(i == 2 * half_items - 1)
            def _():
                far_half(i, 1 - core, i).start()
                far_half(i, core, i + 1).start()

            @pl.when(i < r_count - 1)
            def _():
                a_x(1, r, slot).start()
                pass_a(0, r)

            @pl.when(i == r_count - 1)
            def _():
                a_x(0, r_count - 1, slot).start()

            @pl.when(i == r_count)
            def _():
                a_x(1, r_count - 1, slot).start()

            @pl.when((i >= r_count - 1) & (i < 2 * r_count - 2))
            def _():
                pass_a(1, i - (r_count - 1))

            @pl.when(i == 2 * r_count - 2)
            def _():
                pass_a(0, r_count - 1)
                pass_a(1, r_count - 1)

            @pl.when(((i >= 3) & (i < 7)) | ((i >= 8) & (i < 12)))
            def _():
                first = 2 * i + jnp.where(i < 7, 2, 0)
                pass_w(first)
                pass_w(first + 1)

            @pl.when((i >= LAG) & (i < half_items + LAG))
            def _():
                k = i - LAG
                value = product(0, k // r_count, k % r_count, 0)
                far(k).wait_recv()
                end_out[k] = (value + far_in[k].astype(jnp.float32)).astype(jnp.bfloat16)
                to_end(k).start()

            @pl.when(i >= half_items + half_items // 2)
            def _():
                @pl.when(i == half_items + half_items // 2)
                def _():
                    w_there(2)

                @pl.when(i == 2 * half_items - 1)
                def _():
                    sent(w.at[pl.ds(0, 2), pl.ds(0, (3 * w_chunks - w_chunks // 4) * chunk // 2), :], wy_send)
                    sent(end_out, end_send)
                    drain_early(2)

                f = 2 * (i - half_items - half_items // 2)
                each(2, lambda k: last(f + k))

        each(2 * half_items, step)
        sent(far_out, far_send)

    three_quarters = far_out.at[pl.ds(0, 3 * r_count // 2)]
    sent(three_quarters, fin_send)
    own_quarter = done.at[0, :, 0]
    pltpu.make_async_copy(own_quarter, own_quarter, keep_sem).wait()
    remote(three_quarters, three_quarters, fin_send, fin_recv, partner).wait_recv()


def pair_call(n_dp, n_mp, segment_ids, queries, keys, values, out_weight):
    rows, tokens = queries.shape[0], segment_ids.shape[0]
    depth, width = out_weight.shape
    out_cols = width // n_mp
    quarter = out_cols // 4
    heads = queries.shape[1] // HD
    piece = rows // 4
    count = rows // piece
    items = 2 * count
    dma = pltpu.SemaphoreType.DMA
    hbm = pl.BlockSpec(memory_space=pl.ANY)

    def buffer(*shape):
        return pltpu.VMEM(shape, jnp.bfloat16)

    return pl.pallas_call(
        functools.partial(pair_kernel, n_dp, n_mp, piece),
        out_shape=pltpu.VMEM((rows, out_cols), jnp.bfloat16),
        in_specs=[hbm] * 5,
        out_specs=hbm,
        scratch_shapes=[
            pltpu.VMEM((1, tokens), jnp.int32),
            buffer(rows, heads * HD),
            buffer(2, tokens, HD),
            buffer(n_mp, depth, quarter),
            buffer(n_mp, depth, quarter),
            pltpu.VMEM((rows, tokens), jnp.float32),
            pltpu.VMEM((count, heads * piece, HD), jnp.float32),
            pltpu.VMEM((count, heads * piece, HD), jnp.float32),
            pltpu.VMEM((count, heads * piece, HD), jnp.float32),
            pltpu.VMEM((2 * piece, quarter), jnp.float32),
            buffer(2, 4, rows, depth),
            buffer(2 * items, 2 * piece, quarter), buffer(2 * items, 2 * piece, quarter),
            buffer(items, 2 * piece, quarter), buffer(items, 2 * piece, quarter),
            buffer(2, count, 2, piece, quarter),
            dma((3,)), dma((2,)), dma, dma((4,)), dma, dma((2,)),
            dma, dma((24,)), dma, dma, dma, dma((3,)), dma, dma((count,)),
            dma, dma((count,)), dma, dma((2 * count,)), dma, dma((count,)),
            dma, dma((2 * items + 1,)), dma, dma((items,)), dma, dma, dma,
        ],
        compiler_params=pltpu.CompilerParams(
            collective_id=1, has_side_effects=True, vmem_limit_bytes=60 * 1024 * 1024
        ),
    )(segment_ids.reshape(1, tokens), queries, keys, values, out_weight)


def relay_kernel(
    n_dp, n_mp, key_span, chunk,
    seg_ref, q_ref, k_hbm, v_hbm, w_hbm, out_ref,
    kv, w, bias, attended, from_left, from_right, to_right, to_left,
    load_sems, w_sem, kv_send, kv_recv, pass_send, pass_recv,
    right_send, right_recv, left_send, left_recv,
):
    rows = q_ref.shape[0]
    heads = q_ref.shape[1] // HD
    tokens = n_dp * rows
    out_cols = out_ref.shape[1]
    pieces = out_cols // chunk
    chips = n_dp // 2
    dp, mp = lax.axis_index("dp"), lax.axis_index("mp")
    core, chip = dp % 2, dp // 2
    partner = dp + 1 - 2 * core
    first_row = pl.multiple_of(dp * rows, rows)

    kv_col = pl.multiple_of((mp * heads // GROUP) * HD, HD)
    own = kv.at[:, pl.ds(first_row, rows), :]
    loads = [
        pltpu.make_async_copy(
            src.at[:, pl.ds(kv_col, HD)], kv.at[i, pl.ds(first_row, rows), :], load_sems.at[i]
        )
        for i, src in enumerate((k_hbm, v_hbm))
    ]
    for copy in loads:
        copy.start()
    w_copy = pltpu.make_async_copy(w_hbm, w, w_sem)
    w_copy.start()

    barrier = pltpu.get_barrier_semaphore()
    for r in range(1, chips):
        peer = ((chip + r) % chips) * 2 + core
        pl.semaphore_signal(barrier, inc=1, device_id={"dp": peer}, device_id_type=MESH)
    pl.semaphore_signal(barrier, inc=1, device_id={"dp": partner}, device_id_type=MESH)

    @pl.when(mp > 0)
    def _():
        pl.semaphore_signal(barrier, inc=1, device_id={"mp": mp - 1}, device_id_type=MESH)

    @pl.when(mp < n_mp - 1)
    def _():
        pl.semaphore_signal(barrier, inc=1, device_id={"mp": mp + 1}, device_id_type=MESH)

    ends = jnp.where(mp == 0, 1, 0) + jnp.where(mp == n_mp - 1, 1, 0)
    for copy in loads:
        copy.wait()
    pl.semaphore_wait(barrier, chips + 2 - ends)

    def kv_copy(block, send_sem, recv_sem, target):
        part = kv.at[:, pl.ds(pl.multiple_of(block * rows, rows), rows), :]
        return pltpu.make_async_remote_copy(
            src_ref=part, dst_ref=part, send_sem=send_sem, recv_sem=recv_sem,
            device_id={"dp": target}, device_id_type=MESH,
        )

    sends = [
        kv_copy(dp, kv_send.at[r], kv_recv.at[r], ((chip + r) % chips) * 2 + core)
        for r in range(1, chips)
    ]
    sends.append(kv_copy(dp, pass_send.at[0], pass_recv.at[0], partner))
    for copy in sends:
        copy.start()

    own_segs = seg_ref[:, pl.ds(first_row, rows)].astype(jnp.float32)
    diagonal = lax.broadcasted_iota(jnp.int32, (rows, rows), 0) == lax.broadcasted_iota(
        jnp.int32, (rows, rows), 1
    )
    query_segs = jnp.sum(
        jnp.where(diagonal, jnp.broadcast_to(own_segs, (rows, rows)), 0.0), axis=1, keepdims=True
    )
    for start in range(0, tokens, key_span):
        key_segs = seg_ref[:, start : start + key_span].astype(jnp.float32)
        key_pos = start + lax.broadcasted_iota(jnp.int32, (rows, key_span), 1)
        query_pos = first_row + lax.broadcasted_iota(jnp.int32, (rows, key_span), 0)
        allowed = (query_segs == key_segs) & (key_pos <= query_pos)
        bias[:, start : start + key_span] = jnp.where(allowed, 0.0, -1e30)

    for r in range(1, chips):
        source = ((chip + chips - r) % chips) * 2 + core
        kv_copy(source, kv_send.at[r], kv_recv.at[r], dp).wait_recv()
        forward = kv_copy(source, pass_send.at[r], pass_recv.at[r], partner)
        forward.start()
        sends.append(forward)
    for r in range(chips):
        source = ((chip + chips - r) % chips) * 2 + 1 - core
        kv_copy(source, pass_send.at[r], pass_recv.at[r], dp).wait_recv()

    scale = math.log2(math.e) / math.sqrt(HD)

    def one_head(h, carry):
        columns = pl.ds(pl.multiple_of(h * HD, HD), HD)
        q = q_ref[:, columns]
        top = total = acc = None
        for start in range(0, tokens, key_span):
            span = slice(start, start + key_span)
            scores = lax.dot_general(
                q, kv[0, span, :], (((1,), (1,)), ((), ())), preferred_element_type=jnp.float32
            )
            scores = scores * scale + bias[:, span]
            new_top = jnp.max(scores, axis=1, keepdims=True)
            if top is not None:
                new_top = jnp.maximum(top, new_top)
            probs = jnp.exp2(scores - new_top)
            part_sum = jnp.sum(probs, axis=1, keepdims=True)
            part = jnp.dot(
                probs.astype(jnp.bfloat16), kv[1, span, :], preferred_element_type=jnp.float32
            )
            if top is None:
                total, acc = part_sum, part
            else:
                fade = jnp.exp2(top - new_top)
                total, acc = total * fade + part_sum, acc * fade + part
            top = new_top
        attended[:, columns] = (acc / total).astype(jnp.bfloat16)
        return carry

    lax.fori_loop(0, heads, one_head, 0)
    w_copy.wait()

    def project(d, k):
        columns = pl.ds(pl.multiple_of(d * out_cols + k * chunk, chunk), chunk)
        return jnp.dot(attended[...], w[:, columns], preferred_element_type=jnp.float32)

    def right_copy(d, k):
        at = d * pieces + k
        return pltpu.make_async_remote_copy(
            src_ref=to_right.at[at], dst_ref=from_left.at[at],
            send_sem=right_send.at[at], recv_sem=right_recv.at[at],
            device_id={"mp": mp + 1}, device_id_type=MESH,
        )

    def left_copy(d, k):
        at = d * pieces + k
        return pltpu.make_async_remote_copy(
            src_ref=to_left.at[at], dst_ref=from_right.at[at],
            send_sem=left_send.at[at], recv_sem=left_recv.at[at],
            device_id={"mp": mp - 1}, device_id_type=MESH,
        )

    def relay(d, k, copy_of, staged, arrived, at_end):
        at = d * pieces + k
        value = project(d, k)

        @pl.when(at_end)
        def _():
            staged[at] = value.astype(jnp.bfloat16)

        @pl.when(jnp.logical_not(at_end))
        def _():
            copy_of(d, k).wait_recv()
            staged[at] = (value + arrived[at].astype(jnp.float32)).astype(jnp.bfloat16)

        copy_of(d, k).start()

    items = (n_mp - 1) * pieces

    def step(t, carry):
        right_item = t - LAG * mp
        left_item = t - LAG * (n_mp - 1 - mp)
        right_at = jnp.maximum(right_item, 0)
        left_at = jnp.maximum(left_item, 0)
        right_to = n_mp - 1 - right_at // pieces
        left_to = left_at // pieces

        @pl.when((right_item >= 0) & (right_item < items) & (right_to > mp))
        def _():
            relay(right_to, right_at % pieces, right_copy, to_right, from_left, mp == 0)

        @pl.when((left_item >= 0) & (left_item < items) & (left_to < mp))
        def _():
            relay(left_to, left_at % pieces, left_copy, to_left, from_right, mp == n_mp - 1)

        return carry

    lax.fori_loop(0, items + LAG * (n_mp - 1), step, 0)

    def finish(k, carry):
        at = mp * pieces + k
        columns = pl.ds(pl.multiple_of(k * chunk, chunk), chunk)
        value = project(mp, k)

        @pl.when(mp == 0)
        def _():
            left_copy(mp, k).wait_recv()
            out_ref[:, columns] = (value + from_right[at].astype(jnp.float32)).astype(jnp.bfloat16)

        @pl.when(mp == n_mp - 1)
        def _():
            right_copy(mp, k).wait_recv()
            out_ref[:, columns] = (value + from_left[at].astype(jnp.float32)).astype(jnp.bfloat16)

        @pl.when((mp > 0) & (mp < n_mp - 1))
        def _():
            left_copy(mp, k).wait_recv()
            right_copy(mp, k).wait_recv()
            both = from_left[at].astype(jnp.float32) + from_right[at].astype(jnp.float32)
            out_ref[:, columns] = (value + both).astype(jnp.bfloat16)

        return carry

    lax.fori_loop(0, pieces, finish, 0)

    for copy in sends:
        copy.wait_send()

    def drain(i, carry):
        s, k = i // pieces, i % pieces

        @pl.when(n_mp - 1 - s > mp)
        def _():
            right_copy(n_mp - 1 - s, k).wait_send()

        @pl.when(s < mp)
        def _():
            left_copy(s, k).wait_send()

        return carry

    lax.fori_loop(0, (n_mp - 1) * pieces, drain, 0)


def relay_call(n_dp, n_mp, segment_ids, queries, keys, values, out_weight):
    rows, tokens = queries.shape[0], segment_ids.shape[0]
    depth, width = out_weight.shape
    out_cols = width // n_mp
    chunk = min(256, out_cols)
    slots = n_mp * (out_cols // chunk)
    key_span = min(2048, tokens)
    dma = pltpu.SemaphoreType.DMA
    vmem = pl.BlockSpec(memory_space=pltpu.VMEM)
    hbm = pl.BlockSpec(memory_space=pl.ANY)
    stage = pltpu.VMEM((slots, rows, chunk), jnp.bfloat16)
    return pl.pallas_call(
        functools.partial(relay_kernel, n_dp, n_mp, key_span, chunk),
        out_shape=jax.ShapeDtypeStruct((rows, out_cols), jnp.bfloat16),
        in_specs=[vmem, vmem, hbm, hbm, hbm],
        out_specs=vmem,
        scratch_shapes=[
            pltpu.VMEM((2, tokens, HD), jnp.bfloat16),
            pltpu.VMEM((depth, width), jnp.bfloat16),
            pltpu.VMEM((rows, tokens), jnp.float32),
            pltpu.VMEM((rows, queries.shape[1]), jnp.bfloat16),
            stage, stage, stage, stage,
            dma((2,)), dma,
            dma((n_dp // 2,)), dma((n_dp // 2,)), dma((n_dp // 2,)), dma((n_dp // 2,)),
            dma((slots,)), dma((slots,)), dma((slots,)), dma((slots,)),
        ],
        compiler_params=pltpu.CompilerParams(
            collective_id=0, has_side_effects=True, vmem_limit_bytes=60 * 1024 * 1024
        ),
    )(segment_ids.reshape(1, tokens), queries, keys, values, out_weight)


def solution(mesh):
    n_dp, n_mp = mesh.shape["dp"], mesh.shape["mp"]
    call = pair_call if (n_dp, n_mp) == (8, 4) else relay_call
    on_device = functools.partial(call, n_dp, n_mp)

    return jax.shard_map(
        on_device,
        mesh=mesh,
        in_specs=(P(), P("dp", "mp"), P("dp", None), P("dp", None), P("mp", None)),
        out_specs=P("dp", "mp"),
        check_vma=False,
    )
```
